32 devices in a mesh: date: 2 (over x), strip: 16 (over z, y, core).
Axes of the slice: x: 2, y: 2, z: 4, core: 2. Of those that a mesh axis runs over, the one named last changes fastest.
Arguments:
- slc: bfloat16 [20, 2, 192, 1408], P('date', None, 'strip'), may hold values from -60 to 60
Outputs:
- coherence: float32 [20, 20, 2, 64, 128], P('date', None, None, 'strip')
The draws below stay inside these ranges and needn't reach their ends.
All inputs are finite; a program needn't handle non-finite values.
Results may differ from the reference program's by a relative error of at most 0.0003.
Values may be sent and summed in bfloat16 or wider, within the bound.
No kernel may reach another device: no remote copies, remote signals or barrier semaphores. Data moves between devices by JAX's collectives and lax.ppermute only.
A program may use at most 128 MiB of HBM per device.

```python
import jax
import jax.numpy as jnp
from jax import lax

COLS = 1408
DATES = 20
NROWS = 192


def draw_slc(key, part):
    key_common, key_noise, key_weight = jax.random.split(key, 3)
    common = jax.random.normal(key_common, (1, 2, NROWS, COLS), jnp.float32)
    noise = jax.random.normal(key_noise, (DATES, 2, NROWS, COLS), jnp.float32)
    weight = jax.random.uniform(key_weight, (DATES, 1, 1, 1), jnp.float32, 0.2, 0.9)
    field = weight * common + jnp.sqrt(1.0 - weight * weight) * noise
    field = jnp.clip(field, -6.0, 6.0)
    return field.astype(jnp.bfloat16)


def setup_inputs(seed: int = 0) -> dict:
    seeds = jax.random.split(jax.random.key(seed), 2)
    slc = draw_slc(jax.random.fold_in(seeds[1], 71), 0)
    return {"slc": slc}


EPS = 1e-06

def window(field):
    shape = field.shape
    tri = field.reshape(shape[:-2] + (shape[-2] // 3, 3, shape[-1] // 11, 11)).sum(axis=(-3, -1))
    padded = jnp.pad(tri, [(0, 0)] * (tri.ndim - 1) + [(1, 1)])
    tri = padded[..., :-2] + padded[..., 1:-1] + padded[..., 2:]
    return tri[..., :-2, :] + tri[..., 1:-1, :] + tri[..., 2:, :]

def reference(slc):
    data = jnp.pad(slc.astype(jnp.float32), ((0, 0), (0, 0), (3, 3), (0, 0)))
    real_part = data[:, 0]
    imag_part = data[:, 1]
    scale = lax.rsqrt(window(real_part * real_part + imag_part * imag_part) + EPS)

    def one_date(items):
        row_real, row_imag, row_scale = items
        first = window(row_real[None] * real_part + row_imag[None] * imag_part)
        second = window(row_imag[None] * real_part - row_real[None] * imag_part)
        both = jnp.stack([first, second], axis=1)
        return both * (row_scale[None] * scale)[:, None]
    return lax.map(one_date, (real_part, imag_part, scale))
```

```python
import functools

import jax
import jax.numpy as jnp
from jax import lax
from jax.experimental import pallas as pl
from jax.experimental.pallas import tpu as pltpu
from jax.sharding import PartitionSpec as P

EPS = 1e-06
LANES = 128
CELL = 11
STEPS = 33
VMEM = pltpu.MemorySpace.VMEM


def lane_tables():
    lane = lax.broadcasted_iota(jnp.int32, (8, LANES), 1)
    turn = lax.rem(lane * 3, CELL)
    bits = [(s, (turn & s) != 0) for s in (1, 2, 4, 8)]
    picks = [(lane * CELL + c) & (LANES - 1) for c in range(CELL)]
    return bits, picks


def unpack(dates, pieces, flat):
    def one(d, carry):
        for ref, src, dst in pieces:
            pair = ref[d, src].astype(jnp.float32)
            for m in range(CELL):
                flat[d, m, 2 * dst : 2 * dst + 2, :] = pair[:, m * LANES : (m + 1) * LANES]
        return carry

    lax.fori_loop(0, dates, one, 0)


def regroup(dates, flat, cells):
    bits, picks = lane_tables()

    def one(d, carry):
        for part in range(6):
            sub, ri = part // 2, part % 2
            v = [flat[d, m, pl.ds(part, 8, stride=6), :] for m in range(CELL)]
            for shift, mask in bits:
                v = [jnp.where(mask, v[(t + shift) % CELL], v[t]) for t in range(CELL)]
            for c in range(CELL):
                cells[d, ri, sub * CELL + c] = jnp.take_along_axis(
                    v[(8 * c) % CELL], picks[c], axis=1
                )
        return carry

    lax.fori_loop(0, dates, one, 0)


def box(first, second):
    sub = lax.broadcasted_iota(jnp.int32, (8, LANES), 0)
    lane = lax.broadcasted_iota(jnp.int32, (8, LANES), 1)
    first = first + pltpu.roll(first, 7, 0) + pltpu.roll(first, 6, 0)
    second = pltpu.roll(second, 4, 0) + pltpu.roll(second, 3, 0) + pltpu.roll(second, 2, 0)
    both = jnp.where(sub < 4, first, second)
    left = jnp.where(lane > 0, pltpu.roll(both, 1, 1), 0.0)
    right = jnp.where(lane < LANES - 1, pltpu.roll(both, LANES - 1, 1), 0.0)
    return both + left + right


def scales(dates, cells, out):
    def one(d, carry):
        def step(s, acc):
            re, im = cells[d, 0, s], cells[d, 1, s]
            return acc + re * re + im * im

        acc = lax.fori_loop(0, STEPS, step, jnp.zeros((8, LANES), jnp.float32), unroll=11)
        out[d] = lax.rsqrt(box(acc, acc) + EPS)
        return carry

    lax.fori_loop(0, dates, one, 0)


def products(rows, cols, row_cells, col_cells):
    count = len(rows) * len(cols)

    def step(s, acc):
        a = [row_cells[i, 0, s] for i in rows]
        b = [row_cells[i, 1, s] for i in rows]
        ab = [x + y for x, y in zip(a, b)]
        acc = list(acc)
        at = 0
        for j in cols:
            c, d = col_cells[j, 0, s], col_cells[j, 1, s]
            cd = c - d
            for i in range(len(rows)):
                acc[at] = acc[at] + a[i] * c
                acc[at + 1] = acc[at + 1] + b[i] * d
                acc[at + 2] = acc[at + 2] + ab[i] * cd
                at += 3
        return tuple(acc)

    zero = jnp.zeros((8, LANES), jnp.float32)
    acc = lax.fori_loop(0, STEPS, step, (zero,) * (3 * count), unroll=3)
    at = 0
    for j in cols:
        for i in rows:
            p, q, r = acc[at : at + 3]
            yield i, j, box(p + q, r - p + q)
            at += 3


def own_kernel(dates, x, up, dn, cells, scale, coh, flat):
    rows = x.shape[1]
    pieces = [(up, q, q) for q in range(3)]
    pieces += [(x, q, q + 3) for q in range(rows)]
    pieces += [(dn, q, q + 3 + rows) for q in range(3)]
    unpack(dates, pieces, flat)
    regroup(dates, flat, cells)
    scales(dates, cells, scale)
    sign = jnp.where(lax.broadcasted_iota(jnp.int32, (8, LANES), 0) < 4, 1.0, -1.0)
    half = dates // 2

    def one(n, carry):
        i = 2 * lax.div(n, 2)
        j0 = half * lax.rem(n, 2)

        @pl.when(i < j0 + half)
        def _():
            rows = [i, i + 1]
            cols = [j0 + t for t in range(half)]
            for a, b, both in products(rows, cols, cells, cells):
                both = both * (scale[a] * scale[b])
                coh[a, b] = both
                coh[b, a] = both * sign

        return carry

    lax.fori_loop(0, dates, one, 0)


def cross_kernel(dates, count, *refs):
    parts = refs[: 5 * (count - 1)]
    own, own_scale, own_coh, out, flat, cells, scale = refs[5 * (count - 1) :]
    me = lax.axis_index("date")
    first = me * dates

    def keep(i, carry):
        out[i, pl.ds(first, dates)] = own_coh[i]
        return carry

    lax.fori_loop(0, dates, keep, 0)
    half = dates // 2
    for t in range(1, count):
        head, tail, mid, up, dn = parts[5 * (t - 1) : 5 * t]
        pieces = [(up, q, q) for q in range(3)]
        pieces += [(head, q, q + 3) for q in range(3)]
        pieces += [(mid, q, q + 6) for q in range(mid.shape[1])]
        pieces += [(tail, q, q + 6 + mid.shape[1]) for q in range(3)]
        pieces += [(dn, q, q + 9 + mid.shape[1]) for q in range(3)]
        unpack(dates, pieces, flat)
        regroup(dates, flat, cells)
        scales(dates, cells, scale)
        base = lax.rem(me + count - t, count) * dates

        def one(n, carry):
            i = 2 * lax.div(n, 2)
            j0 = half * lax.rem(n, 2)
            rows = [i, i + 1]
            cols = [j0 + u for u in range(half)]
            for a, b, both in products(rows, cols, own, cells):
                out[a, base + b] = both * (own_scale[a] * scale[b])
            return carry

        lax.fori_loop(0, dates, one, 0)


def per_device(slc):
    dates, _, rows, width = slc.shape
    count = lax.axis_size("date")
    strips = lax.axis_size("strip")
    up_pairs = [(i, i + 1) for i in range(strips - 1)]
    dn_pairs = [(i + 1, i) for i in range(strips - 1)]
    x = jnp.transpose(slc, (0, 2, 1, 3))
    head, mid, tail = x[:, :3], x[:, 3 : rows - 3], x[:, rows - 3 :]
    parts = []
    for t in range(1, count):
        ring = [(i, (i + t) % count) for i in range(count)]
        h = lax.ppermute(head, "date", ring)
        l = lax.ppermute(tail, "date", ring)
        m = lax.ppermute(mid, "date", ring)
        u = lax.ppermute(l, "strip", up_pairs)
        d = lax.ppermute(h, "strip", dn_pairs)
        parts += [h, l, m, u, d]
    up = lax.ppermute(tail, "strip", up_pairs)
    dn = lax.ppermute(head, "strip", dn_pairs)
    f32 = jnp.float32
    vm = pl.BlockSpec(memory_space=VMEM)
    flat = pltpu.VMEM((dates, CELL, 48, LANES), f32)
    cells, scale, coh = pl.pallas_call(
        functools.partial(own_kernel, dates),
        out_shape=(
            jax.ShapeDtypeStruct((dates, 2, STEPS, 8, LANES), f32),
            jax.ShapeDtypeStruct((dates, 8, LANES), f32),
            jax.ShapeDtypeStruct((dates, dates, 8, LANES), f32),
        ),
        in_specs=[vm] * 3,
        out_specs=(vm,) * 3,
        scratch_shapes=[flat],
        compiler_params=pltpu.CompilerParams(vmem_limit_bytes=20 << 20),
        cost_estimate=pl.CostEstimate(flops=80_000_000, bytes_accessed=4_000_000, transcendentals=0),
        name="own_pairs",
    )(x, up, dn)
    out = pl.pallas_call(
        functools.partial(cross_kernel, dates, count),
        out_shape=jax.ShapeDtypeStruct((dates, dates * count, 8, LANES), f32),
        in_specs=[vm] * (len(parts) + 3),
        out_specs=vm,
        scratch_shapes=[
            flat,
            pltpu.VMEM((dates, 2, STEPS, 8, LANES), f32),
            pltpu.VMEM((dates, 8, LANES), f32),
        ],
        compiler_params=pltpu.CompilerParams(vmem_limit_bytes=48 << 20),
        cost_estimate=pl.CostEstimate(flops=150_000_000, bytes_accessed=5_000_000, transcendentals=0),
        name="cross_pairs",
    )(*parts, cells, scale, coh)
    return out.reshape(dates, dates * count, 2, 4, LANES)


def solution(mesh):
    return jax.shard_map(
        per_device,
        mesh=mesh,
        in_specs=(P("date", None, "strip", None),),
        out_specs=P("date", None, None, "strip", None),
        check_vma=False,
    )
```

```python
import functools

import jax
import jax.numpy as jnp
from jax import lax
from jax.experimental import pallas as pl
from jax.experimental.pallas import tpu as pltpu
from jax.sharding import PartitionSpec as P

EPS = 1e-06
LANES = 128
CELL = 11
STEPS = 33
TILE = (8, LANES)
F32 = jnp.float32
VMEM = pltpu.MemorySpace.VMEM


def iota(dim):
    return lax.broadcasted_iota(jnp.int32, TILE, dim)


def put_rows(ref, date, row, flat, q, at):
    pair = ref[date, row].astype(F32)
    for m in range(CELL):
        flat[q, m, at : at + 2, :] = pair[:, m * LANES : (m + 1) * LANES]


def unpack_outer(dates, refs, flat):
    def one(q, carry):
        for half in range(2):
            for e, ref in enumerate(refs):
                for sub in range(3):
                    put_rows(ref, 2 * q + half, sub, flat, q, half * 24 + e * 6 + sub * 2)
        return carry

    lax.fori_loop(0, dates // 2, one, 0)


def unpack_inner(dates, mid, flat, first):
    def one(q, carry):
        for part in range(4):
            date = jnp.minimum(4 * q + part, dates - 1)
            for row in range(6):
                put_rows(mid, date, row, flat, first + q, part * 12 + row * 2)
        return carry

    lax.fori_loop(0, (dates + 3) // 4, one, 0)


def rotate(first, count, flat, cells):
    lane = iota(1)
    turn = lax.rem(lane * 3, CELL)
    bits = [(s, (turn & s) != 0) for s in (1, 2, 4, 8)]

    def one(q, carry):
        for part in range(6):
            v = [flat[q, m, pl.ds(part, 8, stride=6), :] for m in range(CELL)]
            for shift, mask in bits:
                v = [jnp.where(mask, v[(t + shift) % CELL], v[t]) for t in range(CELL)]
            for c in range(CELL):
                cells[q, part % 2, (part // 2) * CELL + c] = v[(8 * c) % CELL]
        return carry

    lax.fori_loop(first, first + count, one, 0)


def place(first, count, cells, spread=None):
    lane = iota(1)
    for c in range(CELL):
        pick = (lane * CELL + c) & (LANES - 1)

        def one(q, carry):
            for ri in range(2):
                for sub in range(3):
                    s = sub * CELL + c
                    v = jnp.take_along_axis(cells[q, ri, s], pick, axis=1)
                    cells[q, ri, s] = v
                    if spread is not None:
                        spread(q, ri, s, v)
            return carry

        lax.fori_loop(first, first + count, one, 0, unroll=count)


def spread_outer(rep):
    low = iota(0) < 4

    def put(q, ri, s, v):
        w = pltpu.roll(v, 4, 0)
        rep[2 * q, ri, s] = jnp.where(low, v, w)
        rep[2 * q + 1, ri, s] = jnp.where(low, w, v)

    return put


def spread_inner(rep, first):
    low = iota(0) < 4
    even = (iota(0) & 2) == 0

    def put(q, ri, s, v):
        a = jnp.where(even, v, pltpu.roll(v, 2, 0))
        b = jnp.where(even, pltpu.roll(v, 6, 0), v)
        c, d = pltpu.roll(a, 4, 0), pltpu.roll(b, 4, 0)
        at = 4 * (q - first)
        rep[at, ri, s] = jnp.where(low, a, c)
        rep[at + 1, ri, s] = jnp.where(low, b, d)
        rep[at + 2, ri, s] = jnp.where(low, c, a)
        rep[at + 3, ri, s] = jnp.where(low, d, b)

    return put


def products(rows, cols, rep, cells):
    count = len(rows) * len(cols)

    def step(s, acc):
        a = [rep[i, 0, s] for i in rows]
        b = [rep[i, 1, s] for i in rows]
        ab = [x + y for x, y in zip(a, b)]
        acc = list(acc)
        at = 0
        for q in cols:
            c, d = cells[q, 0, s], cells[q, 1, s]
            cd = c - d
            for i in range(len(rows)):
                acc[at] = acc[at] + a[i] * c
                acc[at + 1] = acc[at + 1] + b[i] * d
                acc[at + 2] = acc[at + 2] + ab[i] * cd
                at += 3
        return tuple(acc)

    acc = lax.fori_loop(0, STEPS, step, (jnp.zeros(TILE, F32),) * (3 * count), unroll=11)
    at = 0
    for j in range(len(cols)):
        for i in range(len(rows)):
            p, q, r = acc[at : at + 3]
            yield i, j, p + q, r - p + q
            at += 3


def powers(qs, cells):
    def step(s, acc):
        out = []
        for n, q in enumerate(qs):
            c, d = cells[q, 0, s], cells[q, 1, s]
            out.append(acc[n] + c * c + d * d)
        return tuple(out)

    return lax.fori_loop(0, STEPS, step, (jnp.zeros(TILE, F32),) * len(qs), unroll=11)


def put_outer(outer, group, at, first, second):
    low = iota(0) < 4
    pieces = (
        jnp.where(low, first, pltpu.roll(second, 4, 0)),
        jnp.where(low, pltpu.roll(first, 4, 0), second),
    )
    for n, piece in enumerate(pieces):
        p = at + n
        outer[group + p // 4, 8 * (p % 4) : 8 * (p % 4) + 8, :] = piece


def put_inner(inner, group, at, first, second, dates):
    sub = iota(0)

    def merge(x, y, z, w):
        return jnp.where(sub < 4, jnp.where(sub < 2, x, y), jnp.where(sub < 6, z, w))

    roll = pltpu.roll
    pieces = [merge(first, roll(second, 2, 0), roll(first, 2, 0), roll(second, 4, 0))]
    if dates > 2:
        pieces.append(merge(roll(first, 4, 0), roll(second, 6, 0), roll(first, 6, 0), second))
    for n, piece in enumerate(pieces):
        p = at + 2 * n
        inner[group + p // 4, 4 * (p % 4) : 4 * (p % 4) + 8, :] = piece


def window(first, count, outer, inner, sums):
    lane = iota(1)
    left, right = lane > 0, lane < LANES - 1

    def one(g, carry):
        e = [outer[g, pl.ds(x, 8, stride=4), :] for x in range(4)]
        m = [inner[g, pl.ds(x, 8, stride=2), :] for x in range(2)]
        t, u = e[1] + m[0], m[1] + e[2]
        for r, v in enumerate((e[0] + t, t + m[1], m[0] + u, u + e[3])):
            v = (
                v
                + jnp.where(left, pltpu.roll(v, 1, 1), 0.0)
                + jnp.where(right, pltpu.roll(v, LANES - 1, 1), 0.0)
            )
            sums[g, pl.ds(r, 8, stride=4), :] = v
        return carry

    lax.fori_loop(first, first + count, one, 0, unroll=4)


def sum_at(sums, group, p):
    return sums[group + p // 4, 8 * (p % 4) : 8 * (p % 4) + 8, :]


def inner_chunks(dates):
    return [(q, min(4, dates - 4 * q)) for q in range((dates + 3) // 4)]


def inside_kernel(dates, mid, cells, rep, flat):
    ins = (dates + 3) // 4
    unpack_inner(dates, mid, flat, 0)
    rotate(0, ins, flat, cells)
    place(0, ins, cells, spread_inner(rep, 0))


def outside_kernel(dates, head, tail, up, dn, cells, rep, flat):
    outs = dates // 2
    unpack_outer(dates, (up, head, tail, dn), flat)
    rotate(0, outs, flat, cells)
    place(0, outs, cells, spread_outer(rep))


def own_kernel(
    dates, cells_outer, cells_inner, rep_outer, rep_inner, scale, coh, outer, inner, sums
):
    outs = dates // 2
    groups = dates // 2
    sign = jnp.where(iota(0) < 4, 1.0, -1.0)
    for n, pw in enumerate(powers(range(outs), cells_outer)):
        put_outer(outer, outs * groups, 2 * n, pw, pw)
    chunks = inner_chunks(dates)
    for (q, size), pw in zip(chunks, powers([q for q, _ in chunks], cells_inner)):
        put_inner(inner, outs * groups, 4 * q, pw, pw, size)
    for b in range(outs):
        rows = [2 * b, 2 * b + 1]
        cols = list(range(b, outs))
        for i, j, re, im in products(rows, cols, rep_outer, cells_outer):
            put_outer(outer, groups * b, dates * i + 2 * cols[j], re, im)
        picks = [c for c in chunks if 4 * c[0] + c[1] > 2 * b]
        for i, j, re, im in products(rows, [q for q, _ in picks], rep_inner, cells_inner):
            put_inner(inner, groups * b, dates * i + 4 * picks[j][0], re, im, picks[j][1])
    window(0, outs * groups + (dates + 3) // 4, outer, inner, sums)
    for j in range(dates):
        scale[j] = lax.rsqrt(sum_at(sums, outs * groups, j) + EPS)

    for b in range(outs):
        for i in range(2):
            for j in range(2 * b + i, dates):
                v = sum_at(sums, groups * b, dates * i + j) * (scale[2 * b + i] * scale[j])
                coh[2 * b + i, j] = v
                if j != 2 * b + i:
                    coh[j, 2 * b + i] = v * sign


def outer_kernel(dates, rep_outer, head, tail, up, dn, outer, flat, cells):
    outs = dates // 2
    groups = dates // 2
    unpack_outer(dates, (up, head, tail, dn), flat)
    rotate(0, outs, flat, cells)
    place(0, outs, cells)
    for n, pw in enumerate(powers(range(outs), cells)):
        put_outer(outer, outs * groups, 2 * n, pw, pw)

    def one(b, carry):
        rows = [2 * b, 2 * b + 1]
        for i, j, re, im in products(rows, range(outs), rep_outer, cells):
            put_outer(outer, groups * b, dates * i + 2 * j, re, im)
        return carry

    lax.fori_loop(0, outs, one, 0)


def inner_kernel(dates, count, turn, rep_inner, own_scale, mid, outer, before, out, flat, cells, inner, sums):
    outs = dates // 2
    groups = dates // 2
    chunks = inner_chunks(dates)
    me = lax.axis_index("date")
    unpack_inner(dates, mid, flat, 0)
    rotate(0, len(chunks), flat, cells)
    place(0, len(chunks), cells)
    for (q, size), pw in zip(chunks, powers([q for q, _ in chunks], cells)):
        put_inner(inner, outs * groups, 4 * q, pw, pw, size)

    def one(b, carry):
        rows = [2 * b, 2 * b + 1]
        for i, j, re, im in products(rows, range(len(chunks)), rep_inner, cells):
            put_inner(inner, groups * b, dates * i + 4 * j, re, im, chunks[j][1])
        return carry

    lax.fori_loop(0, outs, one, 0)
    window(0, outs * groups + (dates + 3) // 4, outer, inner, sums)
    base = lax.rem(me + count - turn, count) * dates
    scale = [lax.rsqrt(sum_at(sums, outs * groups, j) + EPS) for j in range(dates)]

    def finish(b, carry):
        for i in range(2):
            mine = own_scale[2 * b + i]
            for j in range(dates):
                v = sum_at(sums, groups * b, dates * i + j)
                out[2 * b + i, base + j] = v * (mine * scale[j])
        return carry

    lax.fori_loop(0, outs, finish, 0)
    if turn == 1:

        def keep(i, carry):
            out[i, pl.ds(me * dates, dates)] = before[i]
            return carry

    else:

        def keep(i, carry):
            for t in [0] + list(range(1, turn)):
                at = lax.rem(me + count - t, count) * dates
                out[i, pl.ds(at, dates)] = before[i, pl.ds(at, dates)]
            return carry

    lax.fori_loop(0, dates, keep, 0)


def call(kernel, name, args, outs, scratch=(), flops=0, limit=32):
    vm = pl.BlockSpec(memory_space=VMEM)
    size = sum(a.size * a.dtype.itemsize for a in (*args, *outs))
    return pl.pallas_call(
        kernel,
        out_shape=tuple(outs),
        in_specs=[vm] * len(args),
        out_specs=(vm,) * len(outs),
        scratch_shapes=list(scratch),
        compiler_params=pltpu.CompilerParams(vmem_limit_bytes=limit << 20),
        cost_estimate=pl.CostEstimate(flops=flops, bytes_accessed=size, transcendentals=0),
        name=name,
    )(*args)


def per_device(slc):
    dates, _, rows, width = slc.shape
    count = lax.axis_size("date")
    strips = lax.axis_size("strip")
    up_pairs = [(i, i + 1) for i in range(strips - 1)]
    dn_pairs = [(i + 1, i) for i in range(strips - 1)]
    outs, ins = dates // 2, (dates + 3) // 4
    total = outs * outs + (dates + 3) // 4
    shape = jax.ShapeDtypeStruct

    x = jnp.transpose(slc, (0, 2, 1, 3))
    head, tail, mid = x[:, :3], x[:, rows - 3 :], x[:, 3 : rows - 3]
    heads, tails, mids = [], [], []
    for t in range(1, count):
        ring = [(i, (i + t) % count) for i in range(count)]
        heads.append(lax.ppermute(head, "date", ring))
        tails.append(lax.ppermute(tail, "date", ring))
        mids.append(lax.ppermute(mid, "date", ring))
    up = lax.ppermute(tail, "strip", up_pairs)
    dn = lax.ppermute(head, "strip", dn_pairs)

    def flat(q):
        return pltpu.VMEM((q, CELL, 48, LANES), F32)

    def cell(q):
        return (q, 2, STEPS, *TILE)

    cells_inner, rep_inner = call(
        functools.partial(inside_kernel, dates),
        "inside",
        (mid,),
        (shape(cell(ins), F32), shape(cell(4 * ins), F32)),
        [flat(ins)],
        flops=3_000_000,
    )
    heads, tails, cells_inner = lax.optimization_barrier((heads, tails, cells_inner))
    cells_outer, rep_outer = call(
        functools.partial(outside_kernel, dates),
        "outside",
        (head, tail, up, dn),
        (shape(cell(outs), F32), shape(cell(2 * outs), F32)),
        [flat(outs)],
        flops=3_000_000,
    )
    ups = [lax.ppermute(v, "strip", up_pairs) for v in tails]
    dns = [lax.ppermute(v, "strip", dn_pairs) for v in heads]
    pads = [pltpu.VMEM((total, r, LANES), F32) for r in (32, 16, 32)]
    scale, out = call(
        functools.partial(own_kernel, dates),
        "own_pairs",
        (cells_outer, cells_inner, rep_outer, rep_inner),
        (shape((dates, *TILE), F32), shape((dates, dates, *TILE), F32)),
        pads,
        flops=15_000_000,
    )
    for t in range(1, count):
        (outer,) = call(
            functools.partial(outer_kernel, dates),
            "outer_pairs",
            (rep_outer, heads[t - 1], tails[t - 1], ups[t - 1], dns[t - 1]),
            (shape((total, 32, LANES), F32),),
            [flat(outs), pltpu.VMEM(cell(outs), F32)],
            flops=15_000_000,
        )
        (out,) = call(
            functools.partial(inner_kernel, dates, count, t),
            "inner_pairs",
            (rep_inner, scale, mids[t - 1], outer, out),
            (shape((dates, dates * count, *TILE), F32),),
            [flat(ins), pltpu.VMEM(cell(ins), F32)] + pads[1:],
            flops=15_000_000,
        )
    return out.reshape(dates, dates * count, 2, 4, LANES)


def solution(mesh):
    return jax.shard_map(
        per_device,
        mesh=mesh,
        in_specs=(P("date", None, "strip", None),),
        out_specs=P("date", None, None, "strip", None),
        check_vma=False,
    )
```

```python
import functools

import jax
import jax.numpy as jnp
from jax import lax
from jax.experimental import pallas as pl
from jax.experimental.pallas import tpu as pltpu
from jax.sharding import PartitionSpec as P

EPS = 1e-06
LANES = 128
CELL = 11
STEPS = 33
TILE = (8, LANES)
F32 = jnp.float32
VMEM = pltpu.MemorySpace.VMEM


def iota(dim):
    return lax.broadcasted_iota(jnp.int32, TILE, dim)


def put_rows(ref, date, row, flat, q, at):
    pair = ref[date, row].astype(F32)
    for m in range(CELL):
        flat[q, m, at : at + 2, :] = pair[:, m * LANES : (m + 1) * LANES]


def unpack_outer(dates, refs, flat):
    def one(q, carry):
        for half in range(2):
            for e, ref in enumerate(refs):
                for sub in range(3):
                    put_rows(ref, 2 * q + half, sub, flat, q, half * 24 + e * 6 + sub * 2)
        return carry

    lax.fori_loop(0, dates // 2, one, 0)


def unpack_inner(dates, mid, flat, first):
    def one(q, carry):
        for part in range(4):
            date = jnp.minimum(4 * q + part, dates - 1)
            for row in range(6):
                put_rows(mid, date, row, flat, first + q, part * 12 + row * 2)
        return carry

    lax.fori_loop(0, (dates + 3) // 4, one, 0)


def rotate(first, count, flat, cells):
    lane = iota(1)
    turn = lax.rem(lane * 3, CELL)
    bits = [(s, (turn & s) != 0) for s in (1, 2, 4, 8)]

    def one(q, carry):
        for part in range(6):
            v = [flat[q, m, pl.ds(part, 8, stride=6), :] for m in range(CELL)]
            for shift, mask in bits:
                v = [jnp.where(mask, v[(t + shift) % CELL], v[t]) for t in range(CELL)]
            for c in range(CELL):
                cells[q, part % 2, (part // 2) * CELL + c] = v[(8 * c) % CELL]
        return carry

    lax.fori_loop(first, first + count, one, 0)


def place(first, count, cells, spread=None):
    lane = iota(1)
    for c in range(CELL):
        pick = (lane * CELL + c) & (LANES - 1)

        def one(q, carry):
            for ri in range(2):
                for sub in range(3):
                    s = sub * CELL + c
                    v = jnp.take_along_axis(cells[q, ri, s], pick, axis=1)
                    cells[q, ri, s] = v
                    if spread is not None:
                        spread(q, ri, s, v)
            return carry

        lax.fori_loop(first, first + count, one, 0, unroll=count)


def spread_outer(rep):
    low = iota(0) < 4

    def put(q, ri, s, v):
        w = pltpu.roll(v, 4, 0)
        rep[2 * q, ri, s] = jnp.where(low, v, w)
        rep[2 * q + 1, ri, s] = jnp.where(low, w, v)

    return put


def spread_inner(rep, first):
    low = iota(0) < 4
    even = (iota(0) & 2) == 0

    def put(q, ri, s, v):
        a = jnp.where(even, v, pltpu.roll(v, 2, 0))
        b = jnp.where(even, pltpu.roll(v, 6, 0), v)
        c, d = pltpu.roll(a, 4, 0), pltpu.roll(b, 4, 0)
        at = 4 * (q - first)
        rep[at, ri, s] = jnp.where(low, a, c)
        rep[at + 1, ri, s] = jnp.where(low, b, d)
        rep[at + 2, ri, s] = jnp.where(low, c, a)
        rep[at + 3, ri, s] = jnp.where(low, d, b)

    return put


def products(rows, cols, rep, cells):
    count = len(rows) * len(cols)

    def step(s, acc):
        a = [rep[i, 0, s] for i in rows]
        b = [rep[i, 1, s] for i in rows]
        ab = [x + y for x, y in zip(a, b)]
        acc = list(acc)
        at = 0
        for q in cols:
            c, d = cells[q, 0, s], cells[q, 1, s]
            cd = c - d
            for i in range(len(rows)):
                acc[at] = acc[at] + a[i] * c
                acc[at + 1] = acc[at + 1] + b[i] * d
                acc[at + 2] = acc[at + 2] + ab[i] * cd
                at += 3
        return tuple(acc)

    acc = lax.fori_loop(0, STEPS, step, (jnp.zeros(TILE, F32),) * (3 * count), unroll=11)
    at = 0
    for j in range(len(cols)):
        for i in range(len(rows)):
            p, q, r = acc[at : at + 3]
            yield i, j, p + q, r - p + q
            at += 3


def powers(qs, cells):
    def step(s, acc):
        out = []
        for n, q in enumerate(qs):
            c, d = cells[q, 0, s], cells[q, 1, s]
            out.append(acc[n] + c * c + d * d)
        return tuple(out)

    return lax.fori_loop(0, STEPS, step, (jnp.zeros(TILE, F32),) * len(qs), unroll=11)


def put_outer(outer, group, at, first, second):
    low = iota(0) < 4
    pieces = (
        jnp.where(low, first, pltpu.roll(second, 4, 0)),
        jnp.where(low, pltpu.roll(first, 4, 0), second),
    )
    for n, piece in enumerate(pieces):
        p = at + n
        outer[group + p // 4, 8 * (p % 4) : 8 * (p % 4) + 8, :] = piece


def put_inner(inner, group, at, first, second, dates):
    sub = iota(0)

    def merge(x, y, z, w):
        return jnp.where(sub < 4, jnp.where(sub < 2, x, y), jnp.where(sub < 6, z, w))

    roll = pltpu.roll
    pieces = [merge(first, roll(second, 2, 0), roll(first, 2, 0), roll(second, 4, 0))]
    if dates > 2:
        pieces.append(merge(roll(first, 4, 0), roll(second, 6, 0), roll(first, 6, 0), second))
    for n, piece in enumerate(pieces):
        p = at + 2 * n
        inner[group + p // 4, 4 * (p % 4) : 4 * (p % 4) + 8, :] = piece


def window(first, count, outer, inner, sums):
    lane = iota(1)
    left, right = lane > 0, lane < LANES - 1
    odd = iota(0) * 0 + lax.rem(lax.axis_index("strip"), 2) == 1

    def flip(v):
        n = len(v)
        return [jnp.where(odd, v[r], v[n - 1 - r]) for r in range(n)]

    def one(g, carry):
        e = [outer[g, pl.ds(x, 8, stride=4), :] for x in range(4)]
        m = flip([inner[g, pl.ds(x, 8, stride=2), :] for x in range(2)])
        t, u = e[1] + m[0], m[1] + e[2]
        for r, v in enumerate(flip([e[0] + t, t + m[1], m[0] + u, u + e[3]])):
            v = (
                v
                + jnp.where(left, pltpu.roll(v, 1, 1), 0.0)
                + jnp.where(right, pltpu.roll(v, LANES - 1, 1), 0.0)
            )
            sums[g, pl.ds(r, 8, stride=4), :] = v
        return carry

    lax.fori_loop(first, first + count, one, 0, unroll=4)


def sum_at(sums, group, p):
    return sums[group + p // 4, 8 * (p % 4) : 8 * (p % 4) + 8, :]


def inner_chunks(dates):
    return [(q, min(4, dates - 4 * q)) for q in range((dates + 3) // 4)]


def inside_kernel(dates, mid, rep, inner, flat, cells):
    outs = groups = dates // 2
    chunks = inner_chunks(dates)
    unpack_inner(dates, mid, flat, 0)
    rotate(0, len(chunks), flat, cells)
    place(0, len(chunks), cells, spread_inner(rep, 0))
    for (q, size), pw in zip(chunks, powers([q for q, _ in chunks], cells)):
        put_inner(inner, outs * groups, 4 * q, pw, pw, size)
    for b in range(outs):
        rows = [2 * b, 2 * b + 1]
        picks = [c for c in chunks if 4 * c[0] + c[1] > 2 * b]
        for i, j, re, im in products(rows, [q for q, _ in picks], rep, cells):
            put_inner(inner, groups * b, dates * i + 4 * picks[j][0], re, im, picks[j][1])


def own_kernel(dates, near, far, near_halo, far_halo, inner, rep, scale, coh, flat, cells, outer, sums):
    outs = groups = dates // 2
    sign = jnp.where(iota(0) < 4, 1.0, -1.0)
    unpack_outer(dates, (near_halo, near, far, far_halo), flat)
    rotate(0, outs, flat, cells)
    place(0, outs, cells, spread_outer(rep))
    for n, pw in enumerate(powers(range(outs), cells)):
        put_outer(outer, outs * groups, 2 * n, pw, pw)
    for b in range(outs):
        rows = [2 * b, 2 * b + 1]
        cols = list(range(b, outs))
        for i, j, re, im in products(rows, cols, rep, cells):
            put_outer(outer, groups * b, dates * i + 2 * cols[j], re, im)
    window(0, outs * groups + (dates + 3) // 4, outer, inner, sums)
    for j in range(dates):
        scale[j] = lax.rsqrt(sum_at(sums, outs * groups, j) + EPS)
    for b in range(outs):
        for i in range(2):
            for j in range(2 * b + i, dates):
                v = sum_at(sums, groups * b, dates * i + j) * (scale[2 * b + i] * scale[j])
                coh[2 * b + i, j] = v
                if j != 2 * b + i:
                    coh[j, 2 * b + i] = v * sign


def outer_kernel(dates, rep, near, far, near_halo, far_halo, outer, flat, cells):
    outs = groups = dates // 2
    unpack_outer(dates, (near_halo, near, far, far_halo), flat)
    rotate(0, outs, flat, cells)
    place(0, outs, cells)
    for n, pw in enumerate(powers(range(outs), cells)):
        put_outer(outer, outs * groups, 2 * n, pw, pw)

    def one(b, carry):
        rows = [2 * b, 2 * b + 1]
        for i, j, re, im in products(rows, range(outs), rep, cells):
            put_outer(outer, groups * b, dates * i + 2 * j, re, im)
        return carry

    lax.fori_loop(0, outs, one, 0)


def inner_kernel(dates, count, turn, rep_inner, own_scale, mid, outer, before, out, flat, cells, inner, sums):
    outs = dates // 2
    groups = dates // 2
    chunks = inner_chunks(dates)
    me = lax.axis_index("date")
    unpack_inner(dates, mid, flat, 0)
    rotate(0, len(chunks), flat, cells)
    place(0, len(chunks), cells)
    for (q, size), pw in zip(chunks, powers([q for q, _ in chunks], cells)):
        put_inner(inner, outs * groups, 4 * q, pw, pw, size)

    def one(b, carry):
        rows = [2 * b, 2 * b + 1]
        for i, j, re, im in products(rows, range(len(chunks)), rep_inner, cells):
            put_inner(inner, groups * b, dates * i + 4 * j, re, im, chunks[j][1])
        return carry

    lax.fori_loop(0, outs, one, 0)
    window(0, outs * groups + (dates + 3) // 4, outer, inner, sums)
    base = lax.rem(me + count - turn, count) * dates
    scale = [lax.rsqrt(sum_at(sums, outs * groups, j) + EPS) for j in range(dates)]

    def finish(b, carry):
        for i in range(2):
            mine = own_scale[2 * b + i]
            for j in range(dates):
                v = sum_at(sums, groups * b, dates * i + j)
                out[2 * b + i, base + j] = v * (mine * scale[j])
        return carry

    lax.fori_loop(0, outs, finish, 0)
    if turn == 1:

        def keep(i, carry):
            out[i, pl.ds(me * dates, dates)] = before[i]
            return carry

    else:

        def keep(i, carry):
            for t in [0] + list(range(1, turn)):
                at = lax.rem(me + count - t, count) * dates
                out[i, pl.ds(at, dates)] = before[i, pl.ds(at, dates)]
            return carry

    lax.fori_loop(0, dates, keep, 0)


def call(kernel, name, args, outs, scratch=(), flops=0, limit=32):
    vm = pl.BlockSpec(memory_space=VMEM)
    size = sum(a.size * a.dtype.itemsize for a in (*args, *outs))
    return pl.pallas_call(
        kernel,
        out_shape=tuple(outs),
        in_specs=[vm] * len(args),
        out_specs=(vm,) * len(outs),
        scratch_shapes=list(scratch),
        compiler_params=pltpu.CompilerParams(vmem_limit_bytes=limit << 20),
        cost_estimate=pl.CostEstimate(flops=flops, bytes_accessed=size, transcendentals=0),
        name=name,
    )(*args)


def per_device(slc):
    dates, _, rows, width = slc.shape
    count = lax.axis_size("date")
    strips = lax.axis_size("strip")
    chip = [(i, i ^ 1) for i in range(strips)]
    chips = [(i, i + 1 if i % 2 else i - 1) for i in range(1, strips - 1)]
    outs, ins = dates // 2, (dates + 3) // 4
    total = outs * outs + (dates + 3) // 4
    shape = jax.ShapeDtypeStruct

    def flat(q):
        return pltpu.VMEM((q, CELL, 48, LANES), F32)

    def cell(q):
        return (q, 2, STEPS, *TILE)

    x = jnp.transpose(slc, (0, 2, 1, 3))
    odd = lax.rem(lax.axis_index("strip"), 2)
    near = lax.dynamic_slice_in_dim(x, (1 - odd) * (rows - 3), 3, 1)
    far = lax.dynamic_slice_in_dim(x, odd * (rows - 3), 3, 1)
    mid = x[:, 3 : rows - 3]
    nears, fars, mids = [], [], []
    for t in range(1, count):
        ring = [(i, (i + t) % count) for i in range(count)]
        fars.append(lax.ppermute(far, "date", ring))
        nears.append(lax.ppermute(near, "date", ring))
        mids.append(lax.ppermute(mid, "date", ring))
    rep_inner, own_inner = call(
        functools.partial(inside_kernel, dates),
        "inside",
        (mid,),
        (shape(cell(4 * ins), F32), shape((total, 16, LANES), F32)),
        [flat(ins), pltpu.VMEM(cell(ins), F32)],
        flops=15_000_000,
    )
    fars, own_far, rep_inner = lax.optimization_barrier((fars, far, rep_inner))
    far_halo = lax.ppermute(own_far, "strip", chips)
    far_halos = [lax.ppermute(v, "strip", chips) for v in fars]
    nears, own_near = lax.optimization_barrier((nears, near))
    near_halo = lax.ppermute(own_near, "strip", chip)
    near_halos = [lax.ppermute(v, "strip", chip) for v in nears]
    sums = pltpu.VMEM((total, 32, LANES), F32)
    rep_outer, scale, out = call(
        functools.partial(own_kernel, dates),
        "own_pairs",
        (near, far, near_halo, far_halo, own_inner),
        (
            shape(cell(2 * outs), F32),
            shape((dates, *TILE), F32),
            shape((dates, dates, *TILE), F32),
        ),
        [flat(outs), pltpu.VMEM(cell(outs), F32), sums, sums],
        flops=15_000_000,
    )
    for t in range(1, count):
        (outer,) = call(
            functools.partial(outer_kernel, dates),
            "outer_pairs",
            (rep_outer, nears[t - 1], fars[t - 1], near_halos[t - 1], far_halos[t - 1]),
            (shape((total, 32, LANES), F32),),
            [flat(outs), pltpu.VMEM(cell(outs), F32)],
            flops=15_000_000,
        )
        (out,) = call(
            functools.partial(inner_kernel, dates, count, t),
            "inner_pairs",
            (rep_inner, scale, mids[t - 1], outer, out),
            (shape((dates, dates * count, *TILE), F32),),
            [flat(ins), pltpu.VMEM(cell(ins), F32), pltpu.VMEM((total, 16, LANES), F32), sums],
            flops=15_000_000,
        )
    return out.reshape(dates, dates * count, 2, 4, LANES)


def solution(mesh):
    return jax.shard_map(
        per_device,
        mesh=mesh,
        in_specs=(P("date", None, "strip", None),),
        out_specs=P("date", None, None, "strip", None),
        check_vma=False,
    )
```

```python
import functools

import jax
import jax.numpy as jnp
from jax import lax
from jax.experimental import pallas as pl
from jax.experimental.pallas import tpu as pltpu
from jax.sharding import PartitionSpec as P

EPS = 1e-06
LANES = 128
CELL = 11
STEPS = 33
TILE = (8, LANES)
F32 = jnp.float32
VMEM = pltpu.MemorySpace.VMEM


def iota(dim):
    return lax.broadcasted_iota(jnp.int32, TILE, dim)


def put_rows(ref, date, row, flat, q, at):
    pair = ref[date, row].astype(F32)
    for m in range(CELL):
        flat[q, m, at : at + 2, :] = pair[:, m * LANES : (m + 1) * LANES]


def unpack(dates, refs, flat):
    def one(q, carry):
        for part in range(4):
            date = jnp.minimum(4 * q + part, dates - 1)
            for e, (ref, first) in enumerate(refs):
                for sub in range(3):
                    put_rows(ref, date, first + sub, flat, q, part * 12 + e * 6 + sub * 2)
        return carry

    lax.fori_loop(0, (dates + 3) // 4, one, 0)


def rotate(count, flat, cells):
    lane = iota(1)
    turn = lax.rem(lane * 3, CELL)
    bits = [(s, (turn & s) != 0) for s in (1, 2, 4, 8)]

    def one(q, carry):
        for part in range(6):
            v = [flat[q, m, pl.ds(part, 8, stride=6), :] for m in range(CELL)]
            for shift, mask in bits:
                v = [jnp.where(mask, v[(t + shift) % CELL], v[t]) for t in range(CELL)]
            for c in range(CELL):
                cells[q, part % 2, (part // 2) * CELL + c] = v[(8 * c) % CELL]
        return carry

    lax.fori_loop(0, count, one, 0)


def place(count, cells, rep=None):
    lane = iota(1)
    low = iota(0) < 4
    even = (iota(0) & 2) == 0

    def spread(q, ri, s, v):
        a = jnp.where(even, v, pltpu.roll(v, 2, 0))
        b = jnp.where(even, pltpu.roll(v, 6, 0), v)
        c, d = pltpu.roll(a, 4, 0), pltpu.roll(b, 4, 0)
        rep[4 * q, ri, s] = jnp.where(low, a, c)
        rep[4 * q + 1, ri, s] = jnp.where(low, b, d)
        rep[4 * q + 2, ri, s] = jnp.where(low, c, a)
        rep[4 * q + 3, ri, s] = jnp.where(low, d, b)

    for c in range(CELL):
        pick = (lane * CELL + c) & (LANES - 1)

        def one(q, carry):
            for ri in range(2):
                for sub in range(3):
                    s = sub * CELL + c
                    v = jnp.take_along_axis(cells[q, ri, s], pick, axis=1)
                    cells[q, ri, s] = v
                    if rep is not None:
                        spread(q, ri, s, v)
            return carry

        lax.fori_loop(0, count, one, 0, unroll=count)


def products(rows, cols, rep, cells):
    count = len(rows) * len(cols)

    def step(s, acc):
        a = [rep[i, 0, s] for i in rows]
        b = [rep[i, 1, s] for i in rows]
        ab = [x + y for x, y in zip(a, b)]
        acc = list(acc)
        at = 0
        for q in cols:
            c, d = cells[q, 0, s], cells[q, 1, s]
            cd = c - d
            for i in range(len(rows)):
                acc[at] = acc[at] + a[i] * c
                acc[at + 1] = acc[at + 1] + b[i] * d
                acc[at + 2] = acc[at + 2] + ab[i] * cd
                at += 3
        return tuple(acc)

    acc = lax.fori_loop(0, STEPS, step, (jnp.zeros(TILE, F32),) * (3 * count), unroll=11)
    at = 0
    for j in range(len(cols)):
        for i in range(len(rows)):
            p, q, r = acc[at : at + 3]
            yield i, j, p + q, r - p + q
            at += 3


def powers(qs, cells):
    def step(s, acc):
        out = []
        for n, q in enumerate(qs):
            c, d = cells[q, 0, s], cells[q, 1, s]
            out.append(acc[n] + c * c + d * d)
        return tuple(out)

    return lax.fori_loop(0, STEPS, step, (jnp.zeros(TILE, F32),) * len(qs), unroll=11)


def put(sums, group, at, first, second, dates):
    sub = iota(0)
    roll = pltpu.roll

    def merge(x, y, z, w):
        return jnp.where(sub < 4, jnp.where(sub < 2, x, y), jnp.where(sub < 6, z, w))

    pieces = [merge(first, roll(second, 2, 0), roll(first, 2, 0), roll(second, 4, 0))]
    if dates > 2:
        pieces.append(merge(roll(first, 4, 0), roll(second, 6, 0), roll(first, 6, 0), second))
    for n, piece in enumerate(pieces):
        p = at + 2 * n
        sums[group + p // 4, 4 * (p % 4) : 4 * (p % 4) + 8, :] = piece


def window(first, count, mids, edges, halos, out):
    lane = iota(1)
    left, right = lane > 0, lane < LANES - 1
    odd = iota(0) * 0 + lax.rem(lax.axis_index("strip"), 2) == 1

    def flip(v):
        n = len(v)
        return [jnp.where(odd, v[r], v[n - 1 - r]) for r in range(n)]

    def one(n, carry):
        g = first + n
        m, e, h = ([ref[g, pl.ds(x, 8, stride=2), :] for x in range(2)] for ref in (mids, edges, halos))
        m = flip(m)
        t, u = e[0] + m[0], m[1] + e[1]
        for r, v in enumerate(flip([h[0] + t, t + m[1], m[0] + u, u + h[1]])):
            v = (
                v
                + jnp.where(left, pltpu.roll(v, 1, 1), 0.0)
                + jnp.where(right, pltpu.roll(v, LANES - 1, 1), 0.0)
            )
            out[g, pl.ds(r, 8, stride=4), :] = v
        return carry

    lax.fori_loop(0, count, one, 0, unroll=min(count, 5))


def sum_at(sums, group, p):
    return sums[group + p // 4, 8 * (p % 4) : 8 * (p % 4) + 8, :]


def chunks_of(dates):
    return [(q, min(4, dates - 4 * q)) for q in range((dates + 3) // 4)]


def put_powers(dates, cells, sums):
    chunks = chunks_of(dates)
    for (q, size), pw in zip(chunks, powers([q for q, _ in chunks], cells)):
        put(sums, dates * dates // 4, 4 * q, pw, pw, size)


def regroup(dates, refs, flat, cells, rep=None):
    count = (dates + 3) // 4
    unpack(dates, refs, flat)
    rotate(count, flat, cells)
    place(count, cells, rep)


def own_class(dates, refs, rep, sums, flat, cells):
    outs = dates // 2
    regroup(dates, refs, flat, cells, rep)
    put_powers(dates, cells, sums)
    for b in range(outs):
        rows = [2 * b, 2 * b + 1]
        picks = [c for c in chunks_of(dates) if 4 * c[0] + c[1] > 2 * b]
        for i, j, re, im in products(rows, [q for q, _ in picks], rep, cells):
            put(sums, outs * b, dates * i + 4 * picks[j][0], re, im, picks[j][1])


def cross_block(dates, b, rep, cells, sums):
    chunks = chunks_of(dates)
    for i, j, re, im in products([2 * b, 2 * b + 1], range(len(chunks)), rep, cells):
        put(sums, dates // 2 * b, dates * i + 4 * j, re, im, chunks[j][1])


def own_mid_kernel(dates, mid, rep, sums, flat, cells):
    own_class(dates, ((mid, 0), (mid, 3)), rep, sums, flat, cells)


def own_edge_kernel(dates, near, far, rep, sums, flat, cells):
    own_class(dates, ((near, 0), (far, 0)), rep, sums, flat, cells)


def own_halo_kernel(dates, near, far, mids, edges, rep, scale, coh, flat, cells, halos, out):
    outs = dates // 2
    own_class(dates, ((near, 0), (far, 0)), rep, halos, flat, cells)
    window(0, outs * outs + (dates + 3) // 4, mids, edges, halos, out)
    sign = jnp.where(iota(0) < 4, 1.0, -1.0)
    for j in range(dates):
        scale[j] = lax.rsqrt(sum_at(out, outs * outs, j) + EPS)
    for b in range(outs):
        for i in range(2):
            for j in range(2 * b + i, dates):
                v = sum_at(out, outs * b, dates * i + j) * (scale[2 * b + i] * scale[j])
                coh[2 * b + i, j] = v
                if j != 2 * b + i:
                    coh[j, 2 * b + i] = v * sign


def cross_kernel(dates, rep, near, far, sums, flat, cells):
    regroup(dates, ((near, 0), (far, 0)), flat, cells)
    put_powers(dates, cells, sums)

    def one(b, carry):
        cross_block(dates, b, rep, cells, sums)
        return carry

    lax.fori_loop(0, dates // 2, one, 0)


def last_kernel(
    dates, count, turn, rep, own_scale, mid, edges, halos, before, out, flat, cells, mids, wide, scale, stage, sem
):
    outs = dates // 2
    me = lax.axis_index("date")
    if turn == 1:
        keep = pltpu.make_async_copy(before, out.at[:, pl.ds(me * dates, dates)], sem.at[outs])
        keep.start()
    regroup(dates, ((mid, 0), (mid, 3)), flat, cells)
    put_powers(dates, cells, mids)
    window(outs * outs, (dates + 3) // 4, mids, edges, halos, wide)
    for j in range(dates):
        scale[j] = lax.rsqrt(sum_at(wide, outs * outs, j) + EPS)
    base = lax.rem(me + count - turn, count) * dates

    def copy(b):
        rows = pl.ds(2 * b, 2)
        return pltpu.make_async_copy(stage.at[rows], out.at[rows, pl.ds(base, dates)], sem.at[b])

    def one(b, carry):
        cross_block(dates, b, rep, cells, mids)
        window(outs * b, outs, mids, edges, halos, wide)
        for i in range(2):
            mine = own_scale[2 * b + i]
            for j in range(dates):
                stage[2 * b + i, j] = sum_at(wide, outs * b, dates * i + j) * (mine * scale[j])
        copy(b).start()
        return carry

    lax.fori_loop(0, outs, one, 0)
    for b in range(outs):
        copy(b).wait()
    if turn == 1:
        keep.wait()


def call(kernel, name, args, outs, scratch=(), flops=0, limit=32, hbm=False, aliases=None):
    vm = pl.BlockSpec(memory_space=VMEM)
    far = pl.BlockSpec(memory_space=pltpu.MemorySpace.HBM)
    ins = [vm] * len(args)
    for n in aliases or {}:
        ins[n] = far
    size = sum(a.size * a.dtype.itemsize for a in (*args, *outs))
    return pl.pallas_call(
        kernel,
        out_shape=tuple(outs),
        in_specs=ins,
        out_specs=(far if hbm else vm,) * len(outs),
        scratch_shapes=list(scratch),
        input_output_aliases=aliases or {},
        compiler_params=pltpu.CompilerParams(vmem_limit_bytes=limit << 20),
        cost_estimate=pl.CostEstimate(flops=flops, bytes_accessed=size, transcendentals=0),
        name=name,
    )(*args)


def per_device(slc):
    dates, _, rows, width = slc.shape
    count = lax.axis_size("date")
    strips = lax.axis_size("strip")
    chip = [(i, i ^ 1) for i in range(strips)]
    chips = [(i, i + 1 if i % 2 else i - 1) for i in range(1, strips - 1)]
    groups, quads = dates // 2, (dates + 3) // 4
    total = groups * groups + quads
    shape = jax.ShapeDtypeStruct
    sums = shape((total, 16, LANES), F32)
    rep = shape((4 * quads, 2, STEPS, *TILE), F32)
    flat = pltpu.VMEM((quads, CELL, 48, LANES), F32)
    cells = pltpu.VMEM((quads, 2, STEPS, *TILE), F32)
    wide = pltpu.VMEM((total, 32, LANES), F32)
    scales = shape((dates, *TILE), F32)

    def run(kernel, name, args, outs, scratch=(), **options):
        return call(functools.partial(kernel, dates), name, args, outs, (flat, cells, *scratch), flops=15_000_000, **options)

    x = jnp.transpose(slc, (0, 2, 1, 3))
    odd = lax.rem(lax.axis_index("strip"), 2)
    far = lax.dynamic_slice_in_dim(x, odd * (rows - 3), 3, 1)
    x, far = lax.optimization_barrier((x, far))
    near = lax.dynamic_slice_in_dim(x, (1 - odd) * (rows - 3), 3, 1)
    mid = x[:, 3 : rows - 3]
    near, mid = lax.optimization_barrier((near, mid))
    nears, fars, mids = [], [], []
    for t in range(1, count):
        ring = [(i, (i + t) % count) for i in range(count)]
        fars.append(lax.ppermute(far, "date", ring))
        nears.append(lax.ppermute(near, "date", ring))
        mids.append(lax.ppermute(mid, "date", ring))
    rep_mid, own_mid = run(own_mid_kernel, "own_mid", (mid,), (rep, sums))
    fars, own_far, rep_mid = lax.optimization_barrier((fars, far, rep_mid))
    far_halo = lax.ppermute(own_far, "strip", chips)
    far_halos = [lax.ppermute(v, "strip", chips) for v in fars]
    far_halo, far_halos = lax.optimization_barrier((far_halo, far_halos))
    rep_edge, own_edge = run(own_edge_kernel, "own_edge", (near, own_far), (rep, sums))
    nears, own_near, rep_edge = lax.optimization_barrier((nears, near, rep_edge))
    near_halo = lax.ppermute(own_near, "strip", chip)
    near_halos = [lax.ppermute(v, "strip", chip) for v in nears]
    near_halo, near_halos = lax.optimization_barrier((near_halo, near_halos))
    halo_sums = pltpu.VMEM(sums.shape, F32)
    rep_halo, scale, out = run(
        own_halo_kernel,
        "own_halo",
        (near_halo, far_halo, own_mid, own_edge),
        (rep, scales, shape((dates, dates, *TILE), F32)),
        (halo_sums, wide),
    )
    for t in range(1, count):
        (edge,) = run(cross_kernel, "cross_edge", (rep_edge, nears[t - 1], fars[t - 1]), (sums,))
        (halo,) = run(
            cross_kernel, "cross_halo", (rep_halo, near_halos[t - 1], far_halos[t - 1]), (sums,)
        )
        (out,) = call(
            functools.partial(last_kernel, dates, count, t),
            "cross_mid",
            (rep_mid, scale, mids[t - 1], edge, halo, out),
            (shape((dates, dates * count, *TILE), F32),),
            (
                flat,
                cells,
                halo_sums,
                wide,
                pltpu.VMEM(scales.shape, F32),
                pltpu.VMEM((dates, dates, *TILE), F32),
                pltpu.SemaphoreType.DMA((groups + 1,)),
            ),
            flops=15_000_000,
            hbm=True,
            aliases={5: 0} if t > 1 else None,
        )
    return out.reshape(dates, dates * count, 2, 4, LANES)


def solution(mesh):
    return jax.shard_map(
        per_device,
        mesh=mesh,
        in_specs=(P("date", None, "strip", None),),
        out_specs=P("date", None, None, "strip", None),
        check_vma=False,
    )
```

```python
import functools

import jax
import jax.numpy as jnp
from jax import lax
from jax.experimental import pallas as pl
from jax.experimental.pallas import tpu as pltpu
from jax.sharding import PartitionSpec as P

EPS = 1e-06
LANES = 128
CELL = 11
STEPS = 33
TILE = (8, LANES)
F32 = jnp.float32
VMEM = pltpu.MemorySpace.VMEM


def iota(dim):
    return lax.broadcasted_iota(jnp.int32, TILE, dim)


def put_rows(ref, date, row, flat, q, at):
    pair = ref[date, row].astype(F32)
    for m in range(CELL):
        flat[q, m, at : at + 2, :] = pair[:, m * LANES : (m + 1) * LANES]


def unpack(dates, refs, flat):
    def one(q, carry):
        for part in range(4):
            date = jnp.minimum(4 * q + part, dates - 1)
            for e, (ref, first) in enumerate(refs):
                for sub in range(3):
                    put_rows(ref, date, first + sub, flat, q, part * 12 + e * 6 + sub * 2)
        return carry

    lax.fori_loop(0, (dates + 3) // 4, one, 0)


def rotate(count, flat, cells):
    lane = iota(1)
    turn = lax.rem(lane * 3, CELL)
    bits = [(s, (turn & s) != 0) for s in (1, 2, 4, 8)]

    def one(q, carry):
        for part in range(6):
            v = [flat[q, m, pl.ds(part, 8, stride=6), :] for m in range(CELL)]
            for shift, mask in bits:
                v = [jnp.where(mask, v[(t + shift) % CELL], v[t]) for t in range(CELL)]
            for c in range(CELL):
                cells[q, part % 2, (part // 2) * CELL + c] = v[(8 * c) % CELL]
        return carry

    lax.fori_loop(0, count, one, 0)


def place(count, cells, rep=None):
    lane = iota(1)
    low = iota(0) < 4
    even = (iota(0) & 2) == 0

    def spread(q, ri, s, v):
        a = jnp.where(even, v, pltpu.roll(v, 2, 0))
        b = jnp.where(even, pltpu.roll(v, 6, 0), v)
        c, d = pltpu.roll(a, 4, 0), pltpu.roll(b, 4, 0)
        rep[4 * q, ri, s] = jnp.where(low, a, c)
        rep[4 * q + 1, ri, s] = jnp.where(low, b, d)
        rep[4 * q + 2, ri, s] = jnp.where(low, c, a)
        rep[4 * q + 3, ri, s] = jnp.where(low, d, b)

    for c in range(CELL):
        pick = (lane * CELL + c) & (LANES - 1)

        def one(q, carry):
            for ri in range(2):
                for sub in range(3):
                    s = sub * CELL + c
                    v = jnp.take_along_axis(cells[q, ri, s], pick, axis=1)
                    cells[q, ri, s] = v
                    if rep is not None:
                        spread(q, ri, s, v)
            return carry

        lax.fori_loop(0, count, one, 0, unroll=count)


def products(rows, cols, rep, cells):
    count = len(rows) * len(cols)

    def step(s, acc):
        a = [rep[i, 0, s] for i in rows]
        b = [rep[i, 1, s] for i in rows]
        ab = [x + y for x, y in zip(a, b)]
        acc = list(acc)
        at = 0
        for q in cols:
            c, d = cells[q, 0, s], cells[q, 1, s]
            cd = c - d
            for i in range(len(rows)):
                acc[at] = acc[at] + a[i] * c
                acc[at + 1] = acc[at + 1] + b[i] * d
                acc[at + 2] = acc[at + 2] + ab[i] * cd
                at += 3
        return tuple(acc)

    acc = lax.fori_loop(0, STEPS, step, (jnp.zeros(TILE, F32),) * (3 * count), unroll=11)
    at = 0
    for j in range(len(cols)):
        for i in range(len(rows)):
            p, q, r = acc[at : at + 3]
            yield i, j, p + q, r - p + q
            at += 3


def powers(qs, cells):
    def step(s, acc):
        out = []
        for n, q in enumerate(qs):
            c, d = cells[q, 0, s], cells[q, 1, s]
            out.append(acc[n] + c * c + d * d)
        return tuple(out)

    return lax.fori_loop(0, STEPS, step, (jnp.zeros(TILE, F32),) * len(qs), unroll=11)


def split(first, second):
    even = (iota(0) & 1) == 0
    return (
        jnp.where(even, first, pltpu.roll(second, 1, 0)),
        jnp.where(even, pltpu.roll(first, 7, 0), second),
    )


def odd_strip():
    return iota(0) * 0 + lax.rem(lax.axis_index("strip"), 2) == 1


def put(sums, group, first, second):
    low, high = split(first, second)
    sums[0][group] = low
    sums[1][group] = high
    if len(sums) == 4:
        odd = odd_strip()
        sums[2][group] = jnp.where(odd, low, high)
        sums[3][group] = jnp.where(odd, high, low)


def window(first, count, edges, mids, halos, out):
    lane = iota(1)
    left, right = lane > 0, lane < LANES - 1
    odd = odd_strip()

    def one(n, carry):
        g = first + n
        a, d = (ref[g] for ref in edges)
        b, c = (ref[g] for ref in mids)
        near, far = (ref[g] for ref in halos)
        over, under = jnp.where(odd, near, far), jnp.where(odd, far, near)
        bc = b + c
        for r, v in enumerate((over + (a + b), a + bc, bc + d, (c + d) + under)):
            v = (
                v
                + jnp.where(left, pltpu.roll(v, 1, 1), 0.0)
                + jnp.where(right, pltpu.roll(v, LANES - 1, 1), 0.0)
            )
            out[g, pl.ds(r, 8, stride=4), :] = v
        return carry

    lax.fori_loop(0, count, one, 0, unroll=min(count, 6))


def quads_of(dates):
    return (dates + 3) // 4


def sum_at(out, dates, i, j):
    return out[quads_of(dates) * i + j // 4, 8 * (j % 4) : 8 * (j % 4) + 8, :]


def regroup(dates, refs, flat, cells, rep=None):
    count = quads_of(dates)
    unpack(dates, refs, flat)
    rotate(count, flat, cells)
    place(count, cells, rep)


def put_powers(dates, cells, sums):
    quads = quads_of(dates)
    for q, pw in enumerate(powers(range(quads), cells)):
        put(sums, quads * dates + q, pw, pw)


def own_class(dates, refs, rep, sums, flat, cells):
    quads = quads_of(dates)
    regroup(dates, refs, flat, cells, rep)
    put_powers(dates, cells, sums)
    for b in range(dates // 2):
        picks = range(2 * b // 4, quads)
        for i, j, re, im in products([2 * b, 2 * b + 1], picks, rep, cells):
            put(sums, quads * (2 * b + i) + picks[j], re, im)


def cross_block(dates, b, rep, cells, sums):
    quads = quads_of(dates)
    for i, q, re, im in products([2 * b, 2 * b + 1], range(quads), rep, cells):
        put(sums, quads * (2 * b + i) + q, re, im)


def own_mid_kernel(dates, upper, lower, rep, low, high, flat, cells):
    own_class(dates, ((upper, 0), (lower, 0)), rep, (low, high), flat, cells)


def own_edge_kernel(dates, edge, rep, low, high, near, far, flat, cells):
    own_class(dates, ((edge, 0), (edge, 3)), rep, (low, high, near, far), flat, cells)


def own_final_kernel(dates, a, d, b, c, near, far, scale, coh, out):
    quads = quads_of(dates)
    window(0, quads * (dates + 1), (a, d), (b, c), (near, far), out)
    sign = jnp.where(iota(0) < 4, 1.0, -1.0)
    for j in range(dates):
        scale[j] = lax.rsqrt(sum_at(out, dates, dates, j) + EPS)
    for i in range(dates):
        for j in range(i, dates):
            v = sum_at(out, dates, i, j) * (scale[i] * scale[j])
            coh[i, j] = v
            if j != i:
                coh[j, i] = v * sign


def cross_edge_kernel(dates, rep, edge, low, high, near, far, flat, cells):
    sums = (low, high, near, far)
    regroup(dates, ((edge, 0), (edge, 3)), flat, cells)
    put_powers(dates, cells, sums)

    def one(b, carry):
        cross_block(dates, b, rep, cells, sums)
        return carry

    lax.fori_loop(0, dates // 2, one, 0)


def cross_mid_kernel(dates, rep, upper, lower, low, high, flat, cells):
    sums = (low, high)
    regroup(dates, ((upper, 0), (lower, 0)), flat, cells)
    put_powers(dates, cells, sums)

    def one(b, carry):
        cross_block(dates, b, rep, cells, sums)
        return carry

    lax.fori_loop(0, dates // 2, one, 0)


def last_kernel(dates, count, turn, own_scale, a, d, b, c, near, far, before, out, wide, scale, stage, sem):
    outs = dates // 2
    quads = quads_of(dates)
    me = lax.axis_index("date")
    sources = ((a, d), (b, c), (near, far))
    if turn == 1:
        keep = pltpu.make_async_copy(before, out.at[:, pl.ds(me * dates, dates)], sem.at[outs])
        keep.start()
    window(quads * dates, quads, *sources, wide)
    for j in range(dates):
        scale[j] = lax.rsqrt(sum_at(wide, dates, dates, j) + EPS)
    base = lax.rem(me + count - turn, count) * dates

    def copy(b):
        rows = pl.ds(2 * b, 2)
        return pltpu.make_async_copy(stage.at[rows], out.at[rows, pl.ds(base, dates)], sem.at[b])

    def one(b, carry):
        window(2 * quads * b, 2 * quads, *sources, wide)
        for i in range(2):
            mine = own_scale[2 * b + i]
            for j in range(dates):
                stage[2 * b + i, j] = sum_at(wide, dates, 2 * b + i, j) * (mine * scale[j])
        copy(b).start()
        return carry

    lax.fori_loop(0, outs, one, 0)
    for b in range(outs):
        copy(b).wait()
    if turn == 1:
        keep.wait()


def call(kernel, name, args, outs, scratch=(), flops=0, limit=32, hbm=False, aliases=None):
    vm = pl.BlockSpec(memory_space=VMEM)
    far = pl.BlockSpec(memory_space=pltpu.MemorySpace.HBM)
    ins = [vm] * len(args)
    for n in aliases or {}:
        ins[n] = far
    size = sum(a.size * a.dtype.itemsize for a in (*args, *outs))
    return pl.pallas_call(
        kernel,
        out_shape=tuple(outs),
        in_specs=ins,
        out_specs=(far if hbm else vm,) * len(outs),
        scratch_shapes=list(scratch),
        input_output_aliases=aliases or {},
        compiler_params=pltpu.CompilerParams(vmem_limit_bytes=limit << 20),
        cost_estimate=pl.CostEstimate(flops=flops, bytes_accessed=size, transcendentals=0),
        name=name,
    )(*args)


def per_device(slc):
    dates, _, rows, width = slc.shape
    count = lax.axis_size("date")
    strips = lax.axis_size("strip")
    chip = [(i, i ^ 1) for i in range(strips)]
    chips = [(i, i + 1 if i % 2 else i - 1) for i in range(1, strips - 1)]
    quads = quads_of(dates)
    shape = jax.ShapeDtypeStruct
    sums = shape((quads * (dates + 1), *TILE), F32)
    rep = shape((4 * quads, 2, STEPS, *TILE), F32)
    flat = pltpu.VMEM((quads, CELL, 48, LANES), F32)
    cells = pltpu.VMEM((quads, 2, STEPS, *TILE), F32)
    wide = pltpu.VMEM((quads * (dates + 1), 32, LANES), F32)
    scales = shape((dates, *TILE), F32)
    block = shape((dates, dates, *TILE), F32)

    def run(kernel, name, args, outs, scratch=(flat, cells), **options):
        return call(functools.partial(kernel, dates), name, args, outs, scratch, flops=15_000_000, **options)

    def swap(near, far):
        return lax.ppermute(near, "strip", chip), lax.ppermute(far, "strip", chips)

    x = jnp.transpose(slc, (0, 2, 1, 3))
    triples = x.reshape(dates, rows // 3, 3, 2, width)
    edge = triples[:, :: rows // 3 - 1].reshape(dates, 6, 2, width)
    rings = [[(i, (i + t) % count) for i in range(count)] for t in range(1, count)]
    rows_edge = [lax.ppermute(edge, "date", ring) for ring in rings]
    rep_edge, *own_edges, near, far = run(own_edge_kernel, "own_edge", (edge,), (rep,) + (sums,) * 4)
    x, edge = lax.optimization_barrier((x, edge))
    upper, lower = x[:, 3:6], x[:, 6:9]
    rows_mid = [(lax.ppermute(upper, "date", ring), lax.ppermute(lower, "date", ring)) for ring in rings]
    own_halos = swap(near, far)
    rep_mid, *own_mids = run(own_mid_kernel, "own_mid", (upper, lower), (rep, sums, sums))
    rows_edge, rep_mid = lax.optimization_barrier((rows_edge, rep_mid))
    edges, halos = [], []
    for t in range(1, count):
        *both, near, far = run(cross_edge_kernel, "cross_edge", (rep_edge, rows_edge[t - 1]), (sums,) * 4)
        edges.append(both)
        halos.append(swap(near, far))
    scale, out = run(
        own_final_kernel, "own_final", (*own_edges, *own_mids, *own_halos), (scales, block), (wide,)
    )
    for t in range(1, count):
        inner = run(cross_mid_kernel, "cross_mid", (rep_mid, *rows_mid[t - 1]), (sums, sums))
        (out,) = call(
            functools.partial(last_kernel, dates, count, t),
            "finish",
            (scale, *edges[t - 1], *inner, *halos[t - 1], out),
            (shape((dates, dates * count, *TILE), F32),),
            (
                wide,
                pltpu.VMEM(scales.shape, F32),
                pltpu.VMEM(block.shape, F32),
                pltpu.SemaphoreType.DMA((dates // 2 + 1,)),
            ),
            flops=5_000_000,
            hbm=True,
            aliases={7: 0} if t > 1 else None,
        )
    return out.reshape(dates, dates * count, 2, 4, LANES)


def solution(mesh):
    return jax.shard_map(
        per_device,
        mesh=mesh,
        in_specs=(P("date", None, "strip", None),),
        out_specs=P("date", None, None, "strip", None),
        check_vma=False,
    )
```

```python
import functools

import jax
import jax.numpy as jnp
from jax import lax
from jax.experimental import pallas as pl
from jax.experimental.pallas import tpu as pltpu
from jax.sharding import PartitionSpec as P

EPS = 1e-06
LANES = 128
CELL = 11
STEPS = 33
TILE = (8, LANES)
F32 = jnp.float32
VMEM = pltpu.MemorySpace.VMEM


def iota(dim):
    return lax.broadcasted_iota(jnp.int32, TILE, dim)


def put_rows(ref, date, row, flat, q, at):
    pair = ref[date, row].astype(F32)
    for m in range(CELL):
        flat[q, m, at : at + 2, :] = pair[:, m * LANES : (m + 1) * LANES]


def unpack_mid(dates, mid, flat):
    def one(q, carry):
        for part in range(4):
            date = jnp.minimum(4 * q + part, dates - 1)
            for row in range(6):
                put_rows(mid, date, row, flat, q, part * 12 + row * 2)
        return carry

    lax.fori_loop(0, quads_of(dates), one, 0)


def unpack_edge(dates, own, other, flat):
    for j in range(2 * dates):
        ref, date = (own, j) if j < dates else (other, j - dates)
        for sub in range(3):
            put_rows(ref, date, sub, flat, j // 8, (j % 8) * 6 + sub * 2)


def rotate(count, flat, cells):
    lane = iota(1)
    turn = lax.rem(lane * 3, CELL)
    bits = [(s, (turn & s) != 0) for s in (1, 2, 4, 8)]

    def one(q, carry):
        for part in range(6):
            v = [flat[q, m, pl.ds(part, 8, stride=6), :] for m in range(CELL)]
            for shift, mask in bits:
                v = [jnp.where(mask, v[(t + shift) % CELL], v[t]) for t in range(CELL)]
            for c in range(CELL):
                cells[q, part % 2, (part // 2) * CELL + c] = v[(8 * c) % CELL]
        return carry

    lax.fori_loop(0, count, one, 0)


def place(count, cells, spread=None):
    lane = iota(1)
    for c in range(CELL):
        pick = (lane * CELL + c) & (LANES - 1)

        def one(q, carry):
            for ri in range(2):
                for sub in range(3):
                    s = sub * CELL + c
                    v = jnp.take_along_axis(cells[q, ri, s], pick, axis=1)
                    cells[q, ri, s] = v
                    if spread is not None:
                        spread(q, ri, s, v)
            return carry

        lax.fori_loop(0, count, one, 0, unroll=count)


def spread_mid(rep):
    low = iota(0) < 4
    even = (iota(0) & 2) == 0

    def spread(q, ri, s, v):
        a = jnp.where(even, v, pltpu.roll(v, 2, 0))
        b = jnp.where(even, pltpu.roll(v, 6, 0), v)
        c, d = pltpu.roll(a, 4, 0), pltpu.roll(b, 4, 0)
        rep[4 * q, ri, s] = jnp.where(low, a, c)
        rep[4 * q + 1, ri, s] = jnp.where(low, b, d)
        rep[4 * q + 2, ri, s] = jnp.where(low, c, a)
        rep[4 * q + 3, ri, s] = jnp.where(low, d, b)

    return spread


def spread_edge(dates, cells, rep):
    def one(s, carry):
        for i in range(dates):
            for ri in range(2):
                rep[i, ri, s] = jnp.broadcast_to(cells[i // 8, ri, s, i % 8 : i % 8 + 1, :], TILE)
        return carry

    lax.fori_loop(0, STEPS, one, 0, unroll=3)


def products(rows, cols, rep, cells):
    count = len(rows) * len(cols)

    def step(s, acc):
        a = [rep[i, 0, s] for i in rows]
        b = [rep[i, 1, s] for i in rows]
        ab = [x + y for x, y in zip(a, b)]
        acc = list(acc)
        at = 0
        for q in cols:
            c, d = cells[q, 0, s], cells[q, 1, s]
            cd = c - d
            for i in range(len(rows)):
                acc[at] = acc[at] + a[i] * c
                acc[at + 1] = acc[at + 1] + b[i] * d
                acc[at + 2] = acc[at + 2] + ab[i] * cd
                at += 3
        return tuple(acc)

    acc = lax.fori_loop(0, STEPS, step, (jnp.zeros(TILE, F32),) * (3 * count), unroll=11)
    at = 0
    for j in range(len(cols)):
        for i in range(len(rows)):
            p, q, r = acc[at : at + 3]
            yield i, j, p + q, r - p + q
            at += 3


def powers(qs, cells):
    def step(s, acc):
        out = []
        for n, q in enumerate(qs):
            c, d = cells[q, 0, s], cells[q, 1, s]
            out.append(acc[n] + c * c + d * d)
        return tuple(out)

    return lax.fori_loop(0, STEPS, step, (jnp.zeros(TILE, F32),) * len(qs), unroll=11)


def quads_of(dates):
    return (dates + 3) // 4


def octs_of(dates):
    return (2 * dates + 7) // 8


def edge_kernel(dates, own, other, sums, flat, cells, rep):
    octs = octs_of(dates)
    unpack_edge(dates, own, other, flat)
    rotate(octs, flat, cells)
    place(octs, cells)
    spread_edge(dates, cells, rep)
    for o, pw in enumerate(powers(range(octs), cells)):
        sums[2 * octs * dates + o] = pw

    def one(b, carry):
        for i, o, re, im in products([2 * b, 2 * b + 1], range(octs), rep, cells):
            at = 2 * octs * (2 * b + i) + o
            sums[at] = re
            sums[at + octs] = im
        return carry

    lax.fori_loop(0, dates // 2, one, 0)


def put_mid(dates, rep, cells, sums):
    quads = quads_of(dates)
    for q, pw in enumerate(powers(range(quads), cells)):
        sums[2 * dates, 8 * q : 8 * q + 8, :] = pw

    def one(b, carry):
        for i, q, re, im in products([2 * b, 2 * b + 1], range(quads), rep, cells):
            sums[4 * b + 2 * i, 8 * q : 8 * q + 8, :] = re
            sums[4 * b + 2 * i + 1, 8 * q : 8 * q + 8, :] = im
        return carry

    lax.fori_loop(0, dates // 2, one, 0)


def own_mid_kernel(dates, mid, rep, sums, flat, cells):
    unpack_mid(dates, mid, flat)
    rotate(quads_of(dates), flat, cells)
    place(quads_of(dates), cells, spread_mid(rep))
    put_mid(dates, rep, cells, sums)


def cross_mid_kernel(dates, rep, mid, own, sums, flat, cells, part):
    unpack_mid(dates, mid, flat)
    rotate(quads_of(dates), flat, cells)
    place(quads_of(dates), cells)
    put_mid(dates, rep, cells, part)

    def join(n, carry):
        sums[n, : 2 * dates, :] = own[n, : 2 * dates, :]
        sums[n, 2 * dates : 4 * dates, :] = part[n, : 2 * dates, :]
        return carry

    lax.fori_loop(0, 2 * dates + 1, join, 0, unroll=3)


def window(edges, halos, mids, vreg, mid, octo):
    lane = iota(1)
    odd = iota(0) * 0 + lax.rem(lax.axis_index("strip"), 2) == 1
    near, far = edges[0][vreg], edges[1][vreg]
    near_halo, far_halo = halos[0][vreg], halos[1][vreg]
    a, d = jnp.where(odd, near, far), jnp.where(odd, far, near)
    over, under = jnp.where(odd, near_halo, far_halo), jnp.where(odd, far_halo, near_halo)
    b, c = (mids[mid, pl.ds(16 * octo + e, 8, stride=2), :] for e in range(2))
    bc = b + c
    out = []
    for v in (over + (a + b), a + bc, bc + d, (c + d) + under):
        left = jnp.where(lane > 0, pltpu.roll(v, 1, 1), 0.0)
        right = jnp.where(lane < LANES - 1, pltpu.roll(v, LANES - 1, 1), 0.0)
        out.append(v + left + right)
    return out


def scales(dates, edges, halos, mids, octs, wide, scale):
    total = octs_of(dates)
    for o in octs:
        for r, v in enumerate(window(edges, halos, mids, 2 * total * dates + o, 2 * dates, o)):
            v = lax.rsqrt(v + EPS)
            wide[o, pl.ds(r, 8, stride=8), :] = v
            wide[o, pl.ds(4 + r, 8, stride=8), :] = v
        for j in range(8 * o, min(8 * o + 8, 2 * dates)):
            scale[j] = wide[o, 8 * (j % 8) : 8 * (j % 8) + 8, :]


def sums_of_date(dates, i, edges, halos, mids, octs, wide, at):
    total = octs_of(dates)
    for o in octs:
        for comp in range(2):
            vreg = 2 * total * i + total * comp + o
            for r, v in enumerate(window(edges, halos, mids, vreg, 2 * i + comp, o)):
                wide[at, pl.ds(64 * o + 4 * comp + r, 8, stride=8), :] = v


def early_kernel(dates, near, far, near_halo, far_halo, mids, scale, coh, wide, tall):
    first = min(8, dates)
    edges, halos = (near, far), (near_halo, far_halo)
    scales(dates, edges, halos, mids, range((dates + 7) // 8), wide, scale)

    def one(i, carry):
        sums_of_date(dates, i, edges, halos, mids, [0], tall, i)
        for j in range(first):
            coh[i, j] = tall[i, 8 * j : 8 * j + 8, :] * (scale[i] * scale[j])
        return carry

    lax.fori_loop(0, dates, one, 0, unroll=2)


def last_kernel(
    dates, count, turn, near, far, near_halo, far_halo, mids, before, out, wide, tall, scale, mine, stage, sem
):
    first = min(8, dates)
    octs = octs_of(dates)
    me = lax.axis_index("date")
    base = lax.rem(me + count - turn, count) * dates
    edges, halos = (near, far), (near_halo, far_halo)
    if turn == 1:
        keep = pltpu.make_async_copy(before, out.at[:, pl.ds(me * dates, first)], sem.at[dates])
        keep.start()
    scales(dates, edges, halos, mids, range(octs), wide, scale)

    def copies(b):
        rows = pl.ds(2 * b, 2)
        yield pltpu.make_async_copy(stage.at[rows], out.at[rows, pl.ds(base, dates)], sem.at[b])
        if turn == 1 and dates > first:
            rest = out.at[rows, pl.ds(me * dates + first, dates - first)]
            yield pltpu.make_async_copy(mine.at[rows], rest, sem.at[dates // 2 + b])

    def one(b, carry):
        for i in (2 * b, 2 * b + 1):
            sums_of_date(dates, i, edges, halos, mids, range(1, octs), tall, i)
            for j in range(first, 2 * dates):
                v = tall[i, 8 * j : 8 * j + 8, :] * (scale[i] * scale[j])
                if j < dates:
                    mine[i, j - first] = v
                else:
                    stage[i, j - dates] = v
        for copy in copies(b):
            copy.start()
        return carry

    lax.fori_loop(0, dates // 2, one, 0)
    for b in range(dates // 2):
        for copy in copies(b):
            copy.wait()
    if turn == 1:
        keep.wait()


def call(kernel, name, args, outs, scratch=(), flops=0, limit=32, hbm=False, aliases=None):
    vm = pl.BlockSpec(memory_space=VMEM)
    far = pl.BlockSpec(memory_space=pltpu.MemorySpace.HBM)
    ins = [vm] * len(args)
    for n in aliases or {}:
        ins[n] = far
    size = sum(a.size * a.dtype.itemsize for a in (*args, *outs))
    return pl.pallas_call(
        kernel,
        out_shape=tuple(outs),
        in_specs=ins,
        out_specs=(far if hbm else vm,) * len(outs),
        scratch_shapes=list(scratch),
        input_output_aliases=aliases or {},
        compiler_params=pltpu.CompilerParams(vmem_limit_bytes=limit << 20),
        cost_estimate=pl.CostEstimate(flops=flops, bytes_accessed=size, transcendentals=0),
        name=name,
    )(*args)


def per_device(slc):
    dates, _, rows, width = slc.shape
    count = lax.axis_size("date")
    strips = lax.axis_size("strip")
    chip = [(i, i ^ 1) for i in range(strips)]
    chips = [(i, i + 1 if i % 2 else i - 1) for i in range(1, strips - 1)]
    quads, octs = quads_of(dates), octs_of(dates)
    shape = jax.ShapeDtypeStruct
    edge_sums = shape((octs * (2 * dates + 1), *TILE), F32)
    mid_sums = shape((2 * dates + 1, 16 * ((dates + 7) // 8), LANES), F32)
    all_sums = shape((2 * dates + 1, 16 * octs, LANES), F32)
    rep = shape((4 * quads, 2, STEPS, *TILE), F32)
    wide = pltpu.VMEM((octs, 64, LANES), F32)
    tall = pltpu.VMEM((dates, 64 * octs, LANES), F32)
    first = min(8, dates)
    pairs = shape((dates, first, *TILE), F32)

    def work(n):
        return pltpu.VMEM((n, CELL, 48, LANES), F32), pltpu.VMEM((n, 2, STEPS, *TILE), F32)

    def run(kernel, name, args, outs, scratch):
        return call(functools.partial(kernel, dates), name, args, outs, scratch, flops=15_000_000)

    x = jnp.transpose(slc, (0, 2, 1, 3))
    odd = lax.rem(lax.axis_index("strip"), 2)
    far = lax.dynamic_slice_in_dim(x, odd * (rows - 3), 3, 1)
    x, far = lax.optimization_barrier((x, far))
    near = lax.dynamic_slice_in_dim(x, (1 - odd) * (rows - 3), 3, 1)
    mid = x[:, 3 : rows - 3]
    rings = [[(i, (i + t) % count) for i in range(count)] for t in range(1, count)]
    fars = [lax.ppermute(far, "date", ring) for ring in rings]
    nears = [lax.ppermute(near, "date", ring) for ring in rings]
    middles = [lax.ppermute(mid, "date", ring) for ring in rings]
    rep_mid, own_mid = run(own_mid_kernel, "own_mid", (mid,), (rep, mid_sums), work(quads))
    fars, rep_mid = lax.optimization_barrier((fars, rep_mid))
    edges = []
    for t in range(1, count):
        scratch = (*work(octs), pltpu.VMEM((dates, 2, STEPS, *TILE), F32))
        (far_sums,) = run(edge_kernel, "far_pairs", (far, fars[t - 1]), (edge_sums,), scratch)
        nears[t - 1], far_sums = lax.optimization_barrier((nears[t - 1], far_sums))
        far_halo = lax.ppermute(far_sums, "strip", chips)
        (near_sums,) = run(edge_kernel, "near_pairs", (near, nears[t - 1]), (edge_sums,), scratch)
        near_halo = lax.ppermute(near_sums, "strip", chip)
        edges.append((near_sums, far_sums, near_halo, far_halo))
    _, out = run(
        early_kernel, "early", (*edges[0], own_mid), (shape((8 * ((dates + 7) // 8), *TILE), F32), pairs), (wide, tall)
    )
    middles, out = lax.optimization_barrier((middles, out))
    for t in range(1, count):
        (mids,) = run(
            cross_mid_kernel,
            "cross_mid",
            (rep_mid, middles[t - 1], own_mid),
            (all_sums,),
            (*work(quads), pltpu.VMEM(mid_sums.shape, F32)),
        )
        (out,) = call(
            functools.partial(last_kernel, dates, count, t),
            "finish",
            (*edges[t - 1], mids, out),
            (shape((dates, dates * count, *TILE), F32),),
            (
                wide,
                tall,
                pltpu.VMEM((8 * octs, *TILE), F32),
                pltpu.VMEM((dates, max(1, dates - first), *TILE), F32),
                pltpu.VMEM((dates, dates, *TILE), F32),
                pltpu.SemaphoreType.DMA((dates + 1,)),
            ),
            flops=5_000_000,
            hbm=True,
            aliases={5: 0} if t > 1 else None,
        )
    return out.reshape(dates, dates * count, 2, 4, LANES)


def solution(mesh):
    return jax.shard_map(
        per_device,
        mesh=mesh,
        in_specs=(P("date", None, "strip", None),),
        out_specs=P("date", None, None, "strip", None),
        check_vma=False,
    )
```

```python
import functools

import jax
import jax.numpy as jnp
from jax import lax
from jax.experimental import pallas as pl
from jax.experimental.pallas import tpu as pltpu
from jax.sharding import PartitionSpec as P

EPS = 1e-06
LANES = 128
CELL = 11
STEPS = 33
TILE = (8, LANES)
F32 = jnp.float32
VMEM = pltpu.MemorySpace.VMEM


def iota(dim):
    return lax.broadcasted_iota(jnp.int32, TILE, dim)


def put_rows(ref, date, row, flat, q, at):
    pair = ref[date, row].astype(F32)
    for m in range(CELL):
        flat[q, m, at : at + 2, :] = pair[:, m * LANES : (m + 1) * LANES]


def unpack_mid(dates, mid, flat):
    def one(q, carry):
        for part in range(4):
            date = jnp.minimum(4 * q + part, dates - 1)
            for row in range(6):
                put_rows(mid, date, row, flat, q, part * 12 + row * 2)
        return carry

    lax.fori_loop(0, quads_of(dates), one, 0)


def unpack_edge(dates, own, other, flat):
    for j in range(2 * dates):
        ref, date = (own, j) if j < dates else (other, j - dates)
        for sub in range(3):
            put_rows(ref, date, sub, flat, j // 8, (j % 8) * 6 + sub * 2)


def rotate(count, flat, cells):
    lane = iota(1)
    turn = lax.rem(lane * 3, CELL)
    bits = [(s, (turn & s) != 0) for s in (1, 2, 4, 8)]

    def one(q, carry):
        for part in range(6):
            v = [flat[q, m, pl.ds(part, 8, stride=6), :] for m in range(CELL)]
            for shift, mask in bits:
                v = [jnp.where(mask, v[(t + shift) % CELL], v[t]) for t in range(CELL)]
            for c in range(CELL):
                cells[q, part % 2, (part // 2) * CELL + c] = v[(8 * c) % CELL]
        return carry

    lax.fori_loop(0, count, one, 0)


def place(count, cells, spread=None):
    lane = iota(1)
    for c in range(CELL):
        pick = (lane * CELL + c) & (LANES - 1)

        def one(q, carry):
            for ri in range(2):
                for sub in range(3):
                    s = sub * CELL + c
                    v = jnp.take_along_axis(cells[q, ri, s], pick, axis=1)
                    cells[q, ri, s] = v
                    if spread is not None:
                        spread(q, ri, s, v)
            return carry

        lax.fori_loop(0, count, one, 0, unroll=count)


def spread_mid(rep):
    low = iota(0) < 4
    even = (iota(0) & 2) == 0

    def spread(q, ri, s, v):
        a = jnp.where(even, v, pltpu.roll(v, 2, 0))
        b = jnp.where(even, pltpu.roll(v, 6, 0), v)
        c, d = pltpu.roll(a, 4, 0), pltpu.roll(b, 4, 0)
        rep[4 * q, ri, s] = jnp.where(low, a, c)
        rep[4 * q + 1, ri, s] = jnp.where(low, b, d)
        rep[4 * q + 2, ri, s] = jnp.where(low, c, a)
        rep[4 * q + 3, ri, s] = jnp.where(low, d, b)

    return spread


def spread_edge(dates, cells, rep):
    def one(s, carry):
        for i in range(dates):
            for ri in range(2):
                rep[i, ri, s] = jnp.broadcast_to(cells[i // 8, ri, s, i % 8 : i % 8 + 1, :], TILE)
        return carry

    lax.fori_loop(0, STEPS, one, 0, unroll=3)


def products(rows, cols, rep, cells):
    count = len(rows) * len(cols)

    def step(s, acc):
        a = [rep[i, 0, s] for i in rows]
        b = [rep[i, 1, s] for i in rows]
        ab = [x + y for x, y in zip(a, b)]
        acc = list(acc)
        at = 0
        for q in cols:
            c, d = cells[q, 0, s], cells[q, 1, s]
            cd = c - d
            for i in range(len(rows)):
                acc[at] = acc[at] + a[i] * c
                acc[at + 1] = acc[at + 1] + b[i] * d
                acc[at + 2] = acc[at + 2] + ab[i] * cd
                at += 3
        return tuple(acc)

    acc = lax.fori_loop(0, STEPS, step, (jnp.zeros(TILE, F32),) * (3 * count), unroll=11)
    at = 0
    for j in range(len(cols)):
        for i in range(len(rows)):
            p, q, r = acc[at : at + 3]
            yield i, j, p + q, r - p + q
            at += 3


def powers(qs, cells):
    def step(s, acc):
        out = []
        for n, q in enumerate(qs):
            c, d = cells[q, 0, s], cells[q, 1, s]
            out.append(acc[n] + c * c + d * d)
        return tuple(out)

    return lax.fori_loop(0, STEPS, step, (jnp.zeros(TILE, F32),) * len(qs), unroll=11)


def quads_of(dates):
    return (dates + 3) // 4


def octs_of(dates):
    return (2 * dates + 7) // 8


def edge_kernel(dates, own, other, sums, flat, cells, rep):
    octs = octs_of(dates)
    unpack_edge(dates, own, other, flat)
    rotate(octs, flat, cells)
    place(octs, cells)
    spread_edge(dates, cells, rep)
    for o, pw in enumerate(powers(range(octs), cells)):
        sums[2 * octs * dates + o] = pw

    def one(b, carry):
        for i, o, re, im in products([2 * b, 2 * b + 1], range(octs), rep, cells):
            at = 2 * octs * (2 * b + i) + o
            sums[at] = re
            sums[at + octs] = im
        return carry

    lax.fori_loop(0, dates // 2, one, 0)


def put_mid(dates, rep, cells, sums):
    quads = quads_of(dates)
    for q, pw in enumerate(powers(range(quads), cells)):
        sums[2 * dates, 8 * q : 8 * q + 8, :] = pw

    def one(b, carry):
        for i, q, re, im in products([2 * b, 2 * b + 1], range(quads), rep, cells):
            sums[4 * b + 2 * i, 8 * q : 8 * q + 8, :] = re
            sums[4 * b + 2 * i + 1, 8 * q : 8 * q + 8, :] = im
        return carry

    lax.fori_loop(0, dates // 2, one, 0)


def own_mid_kernel(dates, mid, rep, sums, flat, cells):
    unpack_mid(dates, mid, flat)
    rotate(quads_of(dates), flat, cells)
    place(quads_of(dates), cells, spread_mid(rep))
    put_mid(dates, rep, cells, sums)


def cross_mid_kernel(dates, rep, mid, own, sums, flat, cells, part):
    unpack_mid(dates, mid, flat)
    rotate(quads_of(dates), flat, cells)
    place(quads_of(dates), cells)
    put_mid(dates, rep, cells, part)

    def join(n, carry):
        sums[n, : 2 * dates, :] = own[n, : 2 * dates, :]
        sums[n, 2 * dates : 4 * dates, :] = part[n, : 2 * dates, :]
        return carry

    lax.fori_loop(0, 2 * dates + 1, join, 0, unroll=3)


def window(edges, halos, mids, vreg, mid, octo):
    lane = iota(1)
    odd = iota(0) * 0 + lax.rem(lax.axis_index("strip"), 2) == 1
    near, far = edges[0][vreg], edges[1][vreg]
    near_halo, far_halo = halos[0][vreg], halos[1][vreg]
    a, d = jnp.where(odd, near, far), jnp.where(odd, far, near)
    over, under = jnp.where(odd, near_halo, far_halo), jnp.where(odd, far_halo, near_halo)
    b, c = (mids[mid, pl.ds(16 * octo + e, 8, stride=2), :] for e in range(2))
    bc = b + c
    out = []
    for v in (over + (a + b), a + bc, bc + d, (c + d) + under):
        left = jnp.where(lane > 0, pltpu.roll(v, 1, 1), 0.0)
        right = jnp.where(lane < LANES - 1, pltpu.roll(v, LANES - 1, 1), 0.0)
        out.append(v + left + right)
    return out


def scales(dates, edges, halos, mids, octs, wide, scale):
    total = octs_of(dates)
    for o in octs:
        for r, v in enumerate(window(edges, halos, mids, 2 * total * dates + o, 2 * dates, o)):
            v = lax.rsqrt(v + EPS)
            wide[o, pl.ds(r, 8, stride=8), :] = v
            wide[o, pl.ds(4 + r, 8, stride=8), :] = v
        for j in range(8 * o, min(8 * o + 8, 2 * dates)):
            scale[j] = wide[o, 8 * (j % 8) : 8 * (j % 8) + 8, :]


def sums_of_date(dates, i, edges, halos, mids, octs, wide, at):
    total = octs_of(dates)
    for o in octs:
        for comp in range(2):
            vreg = 2 * total * i + total * comp + o
            for r, v in enumerate(window(edges, halos, mids, vreg, 2 * i + comp, o)):
                wide[at, pl.ds(64 * o + 4 * comp + r, 8, stride=8), :] = v


def early_kernel(dates, near, far, near_halo, far_halo, mids, scale, coh, wide, tall):
    first = min(8, dates)
    edges, halos = (near, far), (near_halo, far_halo)
    scales(dates, edges, halos, mids, range((dates + 7) // 8), wide, scale)

    def one(i, carry):
        sums_of_date(dates, i, edges, halos, mids, [0], tall, i)
        for j in range(first):
            coh[i, j] = tall[i, 8 * j : 8 * j + 8, :] * (scale[i] * scale[j])
        return carry

    lax.fori_loop(0, dates, one, 0, unroll=2)


def last_kernel(
    dates, count, turn, near, far, near_halo, far_halo, mids, before, out, wide, tall, scale, mine, stage, sem
):
    first = min(8, dates)
    octs = octs_of(dates)
    me = lax.axis_index("date")
    base = lax.rem(me + count - turn, count) * dates
    edges, halos = (near, far), (near_halo, far_halo)
    if turn == 1:
        keep = pltpu.make_async_copy(before, out.at[:, pl.ds(me * dates, first)], sem.at[dates])
        keep.start()
    scales(dates, edges, halos, mids, range(octs), wide, scale)

    def copies(b):
        rows = pl.ds(2 * b, 2)
        yield pltpu.make_async_copy(stage.at[rows], out.at[rows, pl.ds(base, dates)], sem.at[b])
        if turn == 1 and dates > first:
            rest = out.at[rows, pl.ds(me * dates + first, dates - first)]
            yield pltpu.make_async_copy(mine.at[rows], rest, sem.at[dates // 2 + b])

    def one(b, carry):
        for i in (2 * b, 2 * b + 1):
            sums_of_date(dates, i, edges, halos, mids, range(1, octs), tall, i)
            for j in range(first, 2 * dates):
                v = tall[i, 8 * j : 8 * j + 8, :] * (scale[i] * scale[j])
                if j < dates:
                    mine[i, j - first] = v
                else:
                    stage[i, j - dates] = v
        for copy in copies(b):
            copy.start()
        return carry

    lax.fori_loop(0, dates // 2, one, 0)
    for b in range(dates // 2):
        for copy in copies(b):
            copy.wait()
    if turn == 1:
        keep.wait()


def call(kernel, name, args, outs, scratch=(), flops=0, limit=32, hbm=False, aliases=None):
    vm = pl.BlockSpec(memory_space=VMEM)
    far = pl.BlockSpec(memory_space=pltpu.MemorySpace.HBM)
    ins = [vm] * len(args)
    for n in aliases or {}:
        ins[n] = far
    size = sum(a.size * a.dtype.itemsize for a in (*args, *outs))
    return pl.pallas_call(
        kernel,
        out_shape=tuple(outs),
        in_specs=ins,
        out_specs=(far if hbm else vm,) * len(outs),
        scratch_shapes=list(scratch),
        input_output_aliases=aliases or {},
        compiler_params=pltpu.CompilerParams(vmem_limit_bytes=limit << 20),
        cost_estimate=pl.CostEstimate(flops=flops, bytes_accessed=size, transcendentals=0),
        name=name,
    )(*args)


def per_device(slc):
    dates, _, rows, width = slc.shape
    count = lax.axis_size("date")
    strips = lax.axis_size("strip")
    chip = [(i, i ^ 1) for i in range(strips)]
    chips = [(i, i + 1 if i % 2 else i - 1) for i in range(1, strips - 1)]
    quads, octs = quads_of(dates), octs_of(dates)
    shape = jax.ShapeDtypeStruct
    edge_sums = shape((octs * (2 * dates + 1), *TILE), F32)
    mid_sums = shape((2 * dates + 1, 16 * ((dates + 7) // 8), LANES), F32)
    all_sums = shape((2 * dates + 1, 16 * octs, LANES), F32)
    rep = shape((4 * quads, 2, STEPS, *TILE), F32)
    wide = pltpu.VMEM((octs, 64, LANES), F32)
    tall = pltpu.VMEM((dates, 64 * octs, LANES), F32)
    first = min(8, dates)
    pairs = shape((dates, first, *TILE), F32)

    def work(n):
        return pltpu.VMEM((n, CELL, 48, LANES), F32), pltpu.VMEM((n, 2, STEPS, *TILE), F32)

    def run(kernel, name, args, outs, scratch):
        return call(functools.partial(kernel, dates), name, args, outs, scratch, flops=15_000_000)

    x = jnp.transpose(slc, (0, 2, 1, 3))
    odd = lax.rem(lax.axis_index("strip"), 2)
    far = lax.dynamic_slice_in_dim(x, odd * (rows - 3), 3, 1)
    x, far = lax.optimization_barrier((x, far))
    near = lax.dynamic_slice_in_dim(x, (1 - odd) * (rows - 3), 3, 1)
    mid = x[:, 3 : rows - 3]
    rings = [[(i, (i + t) % count) for i in range(count)] for t in range(1, count)]
    fars = [lax.ppermute(far, "date", ring) for ring in rings]
    nears = [lax.ppermute(near, "date", ring) for ring in rings]
    middles = [lax.ppermute(mid, "date", ring) for ring in rings]
    edges = []
    for t in range(1, count):
        scratch = (*work(octs), pltpu.VMEM((dates, 2, STEPS, *TILE), F32))
        (far_sums,) = run(edge_kernel, "far_pairs", (far, fars[t - 1]), (edge_sums,), scratch)
        far_halo = lax.ppermute(far_sums, "strip", chips)
        if t == 1:
            own_rows, far_sums = lax.optimization_barrier((mid, far_sums))
            rep_mid, own_mid = run(own_mid_kernel, "own_mid", (own_rows,), (rep, mid_sums), work(quads))
            nears, rep_mid = lax.optimization_barrier((nears, rep_mid))
        (near_sums,) = run(edge_kernel, "near_pairs", (near, nears[t - 1]), (edge_sums,), scratch)
        near_halo = lax.ppermute(near_sums, "strip", chip)
        edges.append((near_sums, far_sums, near_halo, far_halo))
    _, out = run(
        early_kernel, "early", (*edges[0], own_mid), (shape((8 * ((dates + 7) // 8), *TILE), F32), pairs), (wide, tall)
    )
    for t in range(1, count):
        (mids,) = run(
            cross_mid_kernel,
            "cross_mid",
            (rep_mid, middles[t - 1], own_mid),
            (all_sums,),
            (*work(quads), pltpu.VMEM(mid_sums.shape, F32)),
        )
        (out,) = call(
            functools.partial(last_kernel, dates, count, t),
            "finish",
            (*edges[t - 1], mids, out),
            (shape((dates, dates * count, *TILE), F32),),
            (
                wide,
                tall,
                pltpu.VMEM((8 * octs, *TILE), F32),
                pltpu.VMEM((dates, max(1, dates - first), *TILE), F32),
                pltpu.VMEM((dates, dates, *TILE), F32),
                pltpu.SemaphoreType.DMA((dates + 1,)),
            ),
            flops=5_000_000,
            hbm=True,
            aliases={5: 0} if t > 1 else None,
        )
    return out.reshape(dates, dates * count, 2, 4, LANES)


def solution(mesh):
    return jax.shard_map(
        per_device,
        mesh=mesh,
        in_specs=(P("date", None, "strip", None),),
        out_specs=P("date", None, None, "strip", None),
        check_vma=False,
    )
```

```python
import functools

import jax
import jax.numpy as jnp
from jax import lax
from jax.experimental import pallas as pl
from jax.experimental.pallas import tpu as pltpu
from jax.sharding import PartitionSpec as P

EPS = 1e-06
LANES = 128
CELL = 11
STEPS = 33
TILE = (8, LANES)
F32 = jnp.float32
VMEM = pltpu.MemorySpace.VMEM


def iota(dim):
    return lax.broadcasted_iota(jnp.int32, TILE, dim)


def put_rows(ref, date, row, flat, q, at):
    pair = ref[date, row].astype(F32)
    for m in range(CELL):
        flat[q, m, at : at + 2, :] = pair[:, m * LANES : (m + 1) * LANES]


def unpack_mid(dates, mid, flat):
    def one(q, carry):
        for part in range(4):
            date = jnp.minimum(4 * q + part, dates - 1)
            for row in range(6):
                put_rows(mid, date, row, flat, q, part * 12 + row * 2)
        return carry

    lax.fori_loop(0, quads_of(dates), one, 0)


def unpack_edge(dates, own, other, flat):
    for j in range(2 * dates):
        ref, date = (own, j) if j < dates else (other, j - dates)
        for sub in range(3):
            put_rows(ref, date, sub, flat, j // 8, (j % 8) * 6 + sub * 2)


def rotate(count, flat, cells):
    lane = iota(1)
    turn = lax.rem(lane * 3, CELL)
    bits = [(s, (turn & s) != 0) for s in (1, 2, 4, 8)]

    def one(q, carry):
        for part in range(6):
            v = [flat[q, m, pl.ds(part, 8, stride=6), :] for m in range(CELL)]
            for shift, mask in bits:
                v = [jnp.where(mask, v[(t + shift) % CELL], v[t]) for t in range(CELL)]
            for c in range(CELL):
                cells[q, part % 2, (part // 2) * CELL + c] = v[(8 * c) % CELL]
        return carry

    lax.fori_loop(0, count, one, 0)


def place(count, cells, spread=None):
    lane = iota(1)
    for c in range(CELL):
        pick = (lane * CELL + c) & (LANES - 1)

        def one(q, carry):
            for ri in range(2):
                for sub in range(3):
                    s = sub * CELL + c
                    v = jnp.take_along_axis(cells[q, ri, s], pick, axis=1)
                    cells[q, ri, s] = v
                    if spread is not None:
                        spread(q, ri, s, v)
            return carry

        lax.fori_loop(0, count, one, 0, unroll=count)


def spread_mid(rep):
    low = iota(0) < 4
    even = (iota(0) & 2) == 0

    def spread(q, ri, s, v):
        a = jnp.where(even, v, pltpu.roll(v, 2, 0))
        b = jnp.where(even, pltpu.roll(v, 6, 0), v)
        c, d = pltpu.roll(a, 4, 0), pltpu.roll(b, 4, 0)
        rep[4 * q, ri, s] = jnp.where(low, a, c)
        rep[4 * q + 1, ri, s] = jnp.where(low, b, d)
        rep[4 * q + 2, ri, s] = jnp.where(low, c, a)
        rep[4 * q + 3, ri, s] = jnp.where(low, d, b)

    return spread


def products(rows, cols, load, cells):
    count = len(rows) * len(cols)

    def step(s, acc):
        a = [load(i, 0, s) for i in rows]
        b = [load(i, 1, s) for i in rows]
        ab = [x + y for x, y in zip(a, b)]
        acc = list(acc)
        at = 0
        for q in cols:
            c, d = cells[q, 0, s], cells[q, 1, s]
            cd = c - d
            for i in range(len(rows)):
                acc[at] = acc[at] + a[i] * c
                acc[at + 1] = acc[at + 1] + b[i] * d
                acc[at + 2] = acc[at + 2] + ab[i] * cd
                at += 3
        return tuple(acc)

    acc = lax.fori_loop(0, STEPS, step, (jnp.zeros(TILE, F32),) * (3 * count), unroll=11)
    at = 0
    for j in range(len(cols)):
        for i in range(len(rows)):
            p, q, r = acc[at : at + 3]
            yield i, j, p + q, r - p + q
            at += 3


def powers(qs, cells):
    def step(s, acc):
        out = []
        for n, q in enumerate(qs):
            c, d = cells[q, 0, s], cells[q, 1, s]
            out.append(acc[n] + c * c + d * d)
        return tuple(out)

    return lax.fori_loop(0, STEPS, step, (jnp.zeros(TILE, F32),) * len(qs), unroll=11)


def quads_of(dates):
    return (dates + 3) // 4


def octs_of(dates):
    return (2 * dates + 7) // 8


def edge_kernel(dates, own, other, sums, flat, cells):
    octs = octs_of(dates)
    unpack_edge(dates, own, other, flat)
    rotate(octs, flat, cells)
    place(octs, cells)
    for o, pw in enumerate(powers(range(octs), cells)):
        sums[2 * octs * dates + o] = pw

    def load(i, ri, s):
        return cells[i // 8, ri, s, pl.ds(i % 8, 8, stride=0), :]

    for b in range(dates // 2):
        for i, o, re, im in products([2 * b, 2 * b + 1], range(octs), load, cells):
            at = 2 * octs * (2 * b + i) + o
            sums[at] = re
            sums[at + octs] = im


def put_mid(dates, rep, cells, sums):
    quads = quads_of(dates)
    for q, pw in enumerate(powers(range(quads), cells)):
        sums[2 * dates, 8 * q : 8 * q + 8, :] = pw

    def one(b, carry):
        for i, q, re, im in products([2 * b, 2 * b + 1], range(quads), lambda i, ri, s: rep[i, ri, s], cells):
            sums[4 * b + 2 * i, 8 * q : 8 * q + 8, :] = re
            sums[4 * b + 2 * i + 1, 8 * q : 8 * q + 8, :] = im
        return carry

    lax.fori_loop(0, dates // 2, one, 0)


def own_mid_kernel(dates, mid, rep, sums, flat, cells):
    unpack_mid(dates, mid, flat)
    rotate(quads_of(dates), flat, cells)
    place(quads_of(dates), cells, spread_mid(rep))
    put_mid(dates, rep, cells, sums)


def cross_mid_kernel(dates, rep, mid, own, sums, flat, cells, part):
    unpack_mid(dates, mid, flat)
    rotate(quads_of(dates), flat, cells)
    place(quads_of(dates), cells)
    put_mid(dates, rep, cells, part)

    def join(n, carry):
        sums[n, : 2 * dates, :] = own[n, : 2 * dates, :]
        sums[n, 2 * dates : 4 * dates, :] = part[n, : 2 * dates, :]
        return carry

    lax.fori_loop(0, 2 * dates + 1, join, 0, unroll=3)


def window(edges, halos, mids, vreg, mid, octo):
    lane = iota(1)
    odd = iota(0) * 0 + lax.rem(lax.axis_index("strip"), 2) == 1
    near, far = edges[0][vreg], edges[1][vreg]
    near_halo, far_halo = halos[0][vreg], halos[1][vreg]
    a, d = jnp.where(odd, near, far), jnp.where(odd, far, near)
    over, under = jnp.where(odd, near_halo, far_halo), jnp.where(odd, far_halo, near_halo)
    b, c = (mids[mid, pl.ds(16 * octo + e, 8, stride=2), :] for e in range(2))
    bc = b + c
    out = []
    for v in (over + (a + b), a + bc, bc + d, (c + d) + under):
        left = jnp.where(lane > 0, pltpu.roll(v, 1, 1), 0.0)
        right = jnp.where(lane < LANES - 1, pltpu.roll(v, LANES - 1, 1), 0.0)
        out.append(v + left + right)
    return out


def scales(dates, edges, halos, mids, octs, wide, scale):
    total = octs_of(dates)
    for o in octs:
        for r, v in enumerate(window(edges, halos, mids, 2 * total * dates + o, 2 * dates, o)):
            v = lax.rsqrt(v + EPS)
            wide[o, pl.ds(r, 8, stride=8), :] = v
            wide[o, pl.ds(4 + r, 8, stride=8), :] = v
        for j in range(8 * o, min(8 * o + 8, 2 * dates)):
            scale[j] = wide[o, 8 * (j % 8) : 8 * (j % 8) + 8, :]


def sums_of_date(dates, i, edges, halos, mids, octs, wide, at):
    total = octs_of(dates)
    for o in octs:
        for comp in range(2):
            vreg = 2 * total * i + total * comp + o
            for r, v in enumerate(window(edges, halos, mids, vreg, 2 * i + comp, o)):
                wide[at, pl.ds(64 * o + 4 * comp + r, 8, stride=8), :] = v


def early_kernel(dates, near, far, near_halo, far_halo, mids, scale, coh, wide, tall):
    first = min(8, dates)
    edges, halos = (near, far), (near_halo, far_halo)
    scales(dates, edges, halos, mids, range((dates + 7) // 8), wide, scale)

    def one(i, carry):
        sums_of_date(dates, i, edges, halos, mids, [0], tall, i)
        for j in range(first):
            coh[i, j] = tall[i, 8 * j : 8 * j + 8, :] * (scale[i] * scale[j])
        return carry

    lax.fori_loop(0, dates, one, 0, unroll=2)


def last_kernel(
    dates, count, turn, near, far, near_halo, far_halo, mids, before, out, wide, tall, scale, mine, stage, sem
):
    first = min(8, dates)
    octs = octs_of(dates)
    me = lax.axis_index("date")
    base = lax.rem(me + count - turn, count) * dates
    edges, halos = (near, far), (near_halo, far_halo)
    if turn == 1:
        keep = pltpu.make_async_copy(before, out.at[:, pl.ds(me * dates, first)], sem.at[dates])
        keep.start()
    scales(dates, edges, halos, mids, range(octs), wide, scale)

    def copies(b):
        rows = pl.ds(2 * b, 2)
        yield pltpu.make_async_copy(stage.at[rows], out.at[rows, pl.ds(base, dates)], sem.at[b])
        if turn == 1 and dates > first:
            rest = out.at[rows, pl.ds(me * dates + first, dates - first)]
            yield pltpu.make_async_copy(mine.at[rows], rest, sem.at[dates // 2 + b])

    def one(b, carry):
        for i in (2 * b, 2 * b + 1):
            sums_of_date(dates, i, edges, halos, mids, range(1, octs), tall, i)
            for j in range(first, 2 * dates):
                v = tall[i, 8 * j : 8 * j + 8, :] * (scale[i] * scale[j])
                if j < dates:
                    mine[i, j - first] = v
                else:
                    stage[i, j - dates] = v
        for copy in copies(b):
            copy.start()
        return carry

    lax.fori_loop(0, dates // 2, one, 0)
    for b in range(dates // 2):
        for copy in copies(b):
            copy.wait()
    if turn == 1:
        keep.wait()


def call(kernel, name, args, outs, scratch=(), flops=0, limit=32, hbm=False, aliases=None):
    vm = pl.BlockSpec(memory_space=VMEM)
    far = pl.BlockSpec(memory_space=pltpu.MemorySpace.HBM)
    ins = [vm] * len(args)
    for n in aliases or {}:
        ins[n] = far
    size = sum(a.size * a.dtype.itemsize for a in (*args, *outs))
    return pl.pallas_call(
        kernel,
        out_shape=tuple(outs),
        in_specs=ins,
        out_specs=(far if hbm else vm,) * len(outs),
        scratch_shapes=list(scratch),
        input_output_aliases=aliases or {},
        compiler_params=pltpu.CompilerParams(vmem_limit_bytes=limit << 20),
        cost_estimate=pl.CostEstimate(flops=flops, bytes_accessed=size, transcendentals=0),
        name=name,
    )(*args)


def per_device(slc):
    dates, _, rows, width = slc.shape
    count = lax.axis_size("date")
    strips = lax.axis_size("strip")
    chip = [(i, i ^ 1) for i in range(strips)]
    chips = [(i, i + 1 if i % 2 else i - 1) for i in range(1, strips - 1)]
    quads, octs = quads_of(dates), octs_of(dates)
    shape = jax.ShapeDtypeStruct
    edge_sums = shape((octs * (2 * dates + 1), *TILE), F32)
    mid_sums = shape((2 * dates + 1, 16 * ((dates + 7) // 8), LANES), F32)
    all_sums = shape((2 * dates + 1, 16 * octs, LANES), F32)
    rep = shape((4 * quads, 2, STEPS, *TILE), F32)
    wide = pltpu.VMEM((octs, 64, LANES), F32)
    tall = pltpu.VMEM((dates, 64 * octs, LANES), F32)
    first = min(8, dates)
    pairs = shape((dates, first, *TILE), F32)

    def work(n):
        return pltpu.VMEM((n, CELL, 48, LANES), F32), pltpu.VMEM((n, 2, STEPS, *TILE), F32)

    def run(kernel, name, args, outs, scratch):
        return call(functools.partial(kernel, dates), name, args, outs, scratch, flops=15_000_000)

    x = jnp.transpose(slc, (0, 2, 1, 3))
    odd = lax.rem(lax.axis_index("strip"), 2)
    far = lax.dynamic_slice_in_dim(x, odd * (rows - 3), 3, 1)
    x, far = lax.optimization_barrier((x, far))
    near = lax.dynamic_slice_in_dim(x, (1 - odd) * (rows - 3), 3, 1)
    mid = x[:, 3 : rows - 3]
    near, mid = lax.optimization_barrier((near, mid))
    rings = [[(i, (i + t) % count) for i in range(count)] for t in range(1, count)]
    fars = [lax.ppermute(far, "date", ring) for ring in rings]
    nears = [lax.ppermute(near, "date", ring) for ring in rings]
    middles = [lax.ppermute(mid, "date", ring) for ring in rings]
    edges = []
    for t in range(1, count):
        (far_sums,) = run(edge_kernel, "far_pairs", (far, fars[t - 1]), (edge_sums,), work(octs))
        far_halo = lax.ppermute(far_sums, "strip", chips)
        if t == 1:
            own_rows, far_sums = lax.optimization_barrier((mid, far_sums))
            rep_mid, own_mid = run(own_mid_kernel, "own_mid", (own_rows,), (rep, mid_sums), work(quads))
            nears, rep_mid = lax.optimization_barrier((nears, rep_mid))
        (near_sums,) = run(edge_kernel, "near_pairs", (near, nears[t - 1]), (edge_sums,), work(octs))
        near_halo = lax.ppermute(near_sums, "strip", chip)
        edges.append((near_sums, far_sums, near_halo, far_halo))
    _, out = run(
        early_kernel, "early", (*edges[0], own_mid), (shape((8 * ((dates + 7) // 8), *TILE), F32), pairs), (wide, tall)
    )
    for t in range(1, count):
        (mids,) = run(
            cross_mid_kernel,
            "cross_mid",
            (rep_mid, middles[t - 1], own_mid),
            (all_sums,),
            (*work(quads), pltpu.VMEM(mid_sums.shape, F32)),
        )
        (out,) = call(
            functools.partial(last_kernel, dates, count, t),
            "finish",
            (*edges[t - 1], mids, out),
            (shape((dates, dates * count, *TILE), F32),),
            (
                wide,
                tall,
                pltpu.VMEM((8 * octs, *TILE), F32),
                pltpu.VMEM((dates, max(1, dates - first), *TILE), F32),
                pltpu.VMEM((dates, dates, *TILE), F32),
                pltpu.SemaphoreType.DMA((dates + 1,)),
            ),
            flops=5_000_000,
            hbm=True,
            aliases={5: 0} if t > 1 else None,
        )
    return out.reshape(dates, dates * count, 2, 4, LANES)


def solution(mesh):
    return jax.shard_map(
        per_device,
        mesh=mesh,
        in_specs=(P("date", None, "strip", None),),
        out_specs=P("date", None, None, "strip", None),
        check_vma=False,
    )
```

```python
import functools

import jax
import jax.numpy as jnp
from jax import lax
from jax.experimental import pallas as pl
from jax.experimental.pallas import tpu as pltpu
from jax.sharding import PartitionSpec as P

EPS = 1e-06
LANES = 128
CELL = 11
STEPS = 33
TILE = (8, LANES)
F32 = jnp.float32
VMEM = pltpu.MemorySpace.VMEM


def iota(dim):
    return lax.broadcasted_iota(jnp.int32, TILE, dim)


def put_rows(ref, date, row, flat, q, at):
    pair = ref[date, row].astype(F32)
    for m in range(CELL):
        flat[q, m, at : at + 2, :] = pair[:, m * LANES : (m + 1) * LANES]


def unpack_mid(parts, flat):
    first = 0
    for ref in parts:
        dates = ref.shape[0]

        def one(q, carry, ref=ref, dates=dates, first=first):
            for part in range(4):
                date = jnp.minimum(4 * q + part, dates - 1)
                for row in range(6):
                    put_rows(ref, date, row, flat, first + q, part * 12 + row * 2)
            return carry

        lax.fori_loop(0, quads_of(dates), one, 0)
        first += quads_of(dates)
    return first


def unpack_edge(dates, own, other, flat):
    for j in range(2 * dates):
        ref, date = (own, j) if j < dates else (other, j - dates)
        for sub in range(3):
            put_rows(ref, date, sub, flat, j // 8, (j % 8) * 6 + sub * 2)


def rotate(count, flat, cells):
    lane = iota(1)
    turn = lax.rem(lane * 3, CELL)
    bits = [(s, (turn & s) != 0) for s in (1, 2, 4, 8)]

    def one(q, carry):
        for part in range(6):
            v = [flat[q, m, pl.ds(part, 8, stride=6), :] for m in range(CELL)]
            for shift, mask in bits:
                v = [jnp.where(mask, v[(t + shift) % CELL], v[t]) for t in range(CELL)]
            for c in range(CELL):
                cells[q, part % 2, (part // 2) * CELL + c] = v[(8 * c) % CELL]
        return carry

    lax.fori_loop(0, count, one, 0)


def place(count, cells, spread=None):
    lane = iota(1)
    for c in range(CELL):
        pick = (lane * CELL + c) & (LANES - 1)

        def one(q, carry):
            for ri in range(2):
                for sub in range(3):
                    s = sub * CELL + c
                    v = jnp.take_along_axis(cells[q, ri, s], pick, axis=1)
                    cells[q, ri, s] = v
                    if spread is not None:
                        spread(q, ri, s, v)
            return carry

        lax.fori_loop(0, count, one, 0, unroll=count)


def spread_mid(rep):
    low = iota(0) < 4
    even = (iota(0) & 2) == 0

    def spread(q, ri, s, v):
        a = jnp.where(even, v, pltpu.roll(v, 2, 0))
        b = jnp.where(even, pltpu.roll(v, 6, 0), v)
        c, d = pltpu.roll(a, 4, 0), pltpu.roll(b, 4, 0)
        rep[4 * q, ri, s] = jnp.where(low, a, c)
        rep[4 * q + 1, ri, s] = jnp.where(low, b, d)
        rep[4 * q + 2, ri, s] = jnp.where(low, c, a)
        rep[4 * q + 3, ri, s] = jnp.where(low, d, b)

    return spread


def products(rows, cols, load, cells):
    count = len(rows) * len(cols)

    def step(s, acc):
        a = [load(i, 0, s) for i in rows]
        b = [load(i, 1, s) for i in rows]
        ab = [x + y for x, y in zip(a, b)]
        acc = list(acc)
        at = 0
        for q in cols:
            c, d = cells[q, 0, s], cells[q, 1, s]
            cd = c - d
            for i in range(len(rows)):
                acc[at] = acc[at] + a[i] * c
                acc[at + 1] = acc[at + 1] + b[i] * d
                acc[at + 2] = acc[at + 2] + ab[i] * cd
                at += 3
        return tuple(acc)

    acc = lax.fori_loop(0, STEPS, step, (jnp.zeros(TILE, F32),) * (3 * count), unroll=11)
    at = 0
    for j in range(len(cols)):
        for i in range(len(rows)):
            p, q, r = acc[at : at + 3]
            yield i, j, p + q, r - p + q
            at += 3


def powers(qs, cells):
    def step(s, acc):
        out = []
        for n, q in enumerate(qs):
            c, d = cells[q, 0, s], cells[q, 1, s]
            out.append(acc[n] + c * c + d * d)
        return tuple(out)

    return lax.fori_loop(0, STEPS, step, (jnp.zeros(TILE, F32),) * len(qs), unroll=11)


def quads_of(dates):
    return (dates + 3) // 4


def octs_of(dates):
    return (2 * dates + 7) // 8


def edge_kernel(dates, own, other, sums, flat, cells):
    octs = octs_of(dates)
    unpack_edge(dates, own, other, flat)
    rotate(octs, flat, cells)
    place(octs, cells)
    for o, pw in enumerate(powers(range(octs), cells)):
        sums[2 * octs * dates + o] = pw

    def load(i, ri, s):
        return cells[i // 8, ri, s, pl.ds(i % 8, 8, stride=0), :]

    for b in range(dates // 2):
        for i, o, re, im in products([2 * b, 2 * b + 1], range(octs), load, cells):
            at = 2 * octs * (2 * b + i) + o
            sums[at] = re
            sums[at + octs] = im


def near_kernel(dates, own, other, far, mids, sums, rows, flat, cells):
    edge_kernel(dates, own, other, sums, flat, cells)
    middle_rows(dates, 0, sums, far, mids, rows)


def put_mid(dates, quads, rep, cells, sums, first=0, rows=None):
    def store(n, q, v):
        size = 8 if rows is None else min(8, rows - 8 * q)
        sums[n, first + 8 * q : first + 8 * q + size, :] = v[:size]

    for q, pw in enumerate(powers(range(quads), cells)):
        store(2 * dates, q, pw)

    def one(b, carry):
        pairs = products([2 * b, 2 * b + 1], range(quads), lambda i, ri, s: rep[i, ri, s], cells)
        for i, q, re, im in pairs:
            store(4 * b + 2 * i, q, re)
            store(4 * b + 2 * i + 1, q, im)
        return carry

    lax.fori_loop(0, dates // 2, one, 0)


def own_mid_kernel(dates, *refs):
    *parts, rep, sums, flat, cells = refs
    quads = unpack_mid(parts, flat)
    rotate(quads, flat, cells)
    place(quads, cells, spread_mid(rep))
    put_mid(dates, quads, rep, cells, sums)


def cross_mid_kernel(dates, done, ready, rep, mid, before, near, far, sums, *refs):
    rows = refs[: len(ready)]
    flat, cells = refs[len(ready) :]

    def keep(n, carry):
        sums[n, : 2 * (dates + done), :] = before[n, : 2 * (dates + done), :]
        return carry

    quads = unpack_mid([mid], flat)
    rotate(quads, flat, cells)
    place(quads, cells)
    lax.fori_loop(0, 2 * dates + 1, keep, 0, unroll=3)
    put_mid(dates, quads, rep, cells, sums, 2 * (dates + done), 2 * mid.shape[0])
    for o, out in zip(ready, rows):
        middle_rows(dates, o, near, far, sums, out)


def box(v):
    lane = iota(1)
    left = jnp.where(lane > 0, pltpu.roll(v, 1, 1), 0.0)
    right = jnp.where(lane < LANES - 1, pltpu.roll(v, LANES - 1, 1), 0.0)
    return v + left + right


def odd_strip():
    return iota(0) * 0 + lax.rem(lax.axis_index("strip"), 2) == 1


def vreg_of(dates, i, comp, o):
    octs = octs_of(dates)
    if isinstance(i, int) and i == dates:
        return 2 * octs * dates + o
    return 2 * octs * i + octs * comp + o


def mids_of(dates, i, comp, o, mids):
    row = 2 * dates if isinstance(i, int) and i == dates else 2 * i + comp
    return (mids[row, pl.ds(16 * o + e, 8, stride=2), :] for e in range(2))


def each_date(dates, one):
    def step(i, carry):
        one(i)
        return carry

    one(dates)
    lax.fori_loop(0, dates, step, 0, unroll=2)


def middle_rows(dates, o, near, far, mids, out):
    odd = odd_strip()

    def one(i):
        for comp in range(2):
            at = vreg_of(dates, i, comp, o)
            p, q = near[at], far[at]
            b, c = mids_of(dates, i, comp, o, mids)
            a, d = jnp.where(odd, p, q), jnp.where(odd, q, p)
            bc = b + c
            out[i, pl.ds(4 * comp + 1, 8, stride=8), :] = box(a + bc)
            out[i, pl.ds(4 * comp + 2, 8, stride=8), :] = box(bc + d)

    each_date(dates, one)


def outer_row(dates, i, side, sums, halo, mids, out):
    odd = odd_strip()
    for o in range(octs_of(dates)):
        for comp in range(2):
            at = vreg_of(dates, i, comp, o)
            b, c = mids_of(dates, i, comp, o, mids)
            first, second = (b, c) if side == "near" else (c, b)
            v = box(halo[at] + sums[at] + jnp.where(odd, first, second))
            for r in (0, 3):
                out[i, pl.ds(64 * o + 4 * comp + r, 8, stride=8), :] = v


def far_end_kernel(dates, far_halo, far, mids, out):
    each_date(dates, lambda i: outer_row(dates, i, "far", far, far_halo, mids, out))


def last_kernel(dates, count, turn, near_halo, near, mids, far_end, *refs):
    octs = octs_of(dates)
    middle = refs[:octs]
    before, out, ends, scale, mine, other, sem = refs[octs:]
    me = lax.axis_index("date")
    base = lax.rem(me + count - turn, count) * dates
    sub = iota(0) & 3
    odd = odd_strip()
    near_row = sub == jnp.where(odd, 0, 3)
    far_row = sub == jnp.where(odd, 3, 0)

    def tile(i, j):
        o, at = j // 8, 8 * (j % 8)
        rows = slice(8 * j, 8 * j + 8)
        rest = jnp.where(far_row, far_end[i, rows, :], middle[o][i, at : at + 8, :])
        return jnp.where(near_row, ends[i, rows, :], rest)

    outer_row(dates, dates, "near", near, near_halo, mids, ends)
    for j in range(2 * dates):
        scale[j] = lax.rsqrt(tile(dates, j) + EPS)

    def copies(b):
        rows = pl.ds(2 * b, 2)
        yield pltpu.make_async_copy(other.at[rows], out.at[rows, pl.ds(base, dates)], sem.at[b])
        if turn == 1:
            own = out.at[rows, pl.ds(me * dates, dates)]
            yield pltpu.make_async_copy(mine.at[rows], own, sem.at[dates // 2 + b])

    def one(b, carry):
        for i in (2 * b, 2 * b + 1):
            outer_row(dates, i, "near", near, near_halo, mids, ends)
            own = scale[i]
            for j in range(2 * dates):
                v = tile(i, j) * (own * scale[j])
                if j < dates:
                    mine[i, j] = v
                else:
                    other[i, j - dates] = v
        for copy in copies(b):
            copy.start()
        return carry

    lax.fori_loop(0, dates // 2, one, 0)
    for b in range(dates // 2):
        for copy in copies(b):
            copy.wait()


def call(kernel, name, args, outs, scratch=(), flops=0, limit=32, hbm=False, aliases=None):
    vm = pl.BlockSpec(memory_space=VMEM)
    far = pl.BlockSpec(memory_space=pltpu.MemorySpace.HBM)
    ins = [vm] * len(args)
    for n in aliases or {}:
        ins[n] = far
    size = sum(a.size * a.dtype.itemsize for a in (*args, *outs))
    return pl.pallas_call(
        kernel,
        out_shape=tuple(outs),
        in_specs=ins,
        out_specs=(far if hbm else vm,) * len(outs),
        scratch_shapes=list(scratch),
        input_output_aliases=aliases or {},
        compiler_params=pltpu.CompilerParams(vmem_limit_bytes=limit << 20),
        cost_estimate=pl.CostEstimate(flops=flops, bytes_accessed=size, transcendentals=0),
        name=name,
    )(*args)


def per_device(slc):
    dates, _, rows, width = slc.shape
    count = lax.axis_size("date")
    strips = lax.axis_size("strip")
    chip = [(i, i ^ 1) for i in range(strips)]
    chips = [(i, i + 1 if i % 2 else i - 1) for i in range(1, strips - 1)]
    quads, octs = quads_of(dates), octs_of(dates)
    shape = jax.ShapeDtypeStruct
    edge_sums = shape((octs * (2 * dates + 1), *TILE), F32)
    mid_sums = shape((2 * dates + 1, 16 * ((dates + 7) // 8), LANES), F32)
    all_sums = shape((2 * dates + 1, 16 * octs, LANES), F32)
    eight = shape((dates + 1, 64, LANES), F32)
    rep = shape((4 * quads, 2, STEPS, *TILE), F32)

    def work(n):
        return pltpu.VMEM((n, CELL, 48, LANES), F32), pltpu.VMEM((n, 2, STEPS, *TILE), F32)

    def run(kernel, name, args, outs, scratch, fixed=()):
        return call(functools.partial(kernel, dates, *fixed), name, args, outs, scratch, flops=15_000_000)

    x = jnp.transpose(slc, (0, 2, 1, 3))
    odd = lax.rem(lax.axis_index("strip"), 2)
    far = lax.dynamic_slice_in_dim(x, odd * (rows - 3), 3, 1)
    x, far = lax.optimization_barrier((x, far))
    near = lax.dynamic_slice_in_dim(x, (1 - odd) * (rows - 3), 3, 1)
    cuts = [0] + [] + [dates]
    parts = [x[lo:hi, 3 : rows - 3] for lo, hi in zip(cuts, cuts[1:])]
    near, parts = lax.optimization_barrier((near, parts))
    rings = [[(i, (i + t) % count) for i in range(count)] for t in range(1, count)]
    fars = [lax.ppermute(far, "date", ring) for ring in rings]
    nears = [lax.ppermute(near, "date", ring) for ring in rings]
    middles = [[lax.ppermute(part, "date", ring) for part in parts] for ring in rings]
    edges = []
    for t in range(1, count):
        (far_sums,) = run(edge_kernel, "far_pairs", (far, fars[t - 1]), (edge_sums,), work(octs))
        far_halo = lax.ppermute(far_sums, "strip", chips)
        if t == 1:
            own_rows, far_sums = lax.optimization_barrier((parts, far_sums))
            rep_mid, own_mid = run(own_mid_kernel, "own_mid", own_rows, (rep, mid_sums), work(quads))
            nears, rep_mid = lax.optimization_barrier((nears, rep_mid))
        args = (near, nears[t - 1], far_sums, own_mid)
        near_sums, ready = run(near_kernel, "near_pairs", args, (edge_sums, eight), work(octs))
        near_halo = lax.ppermute(near_sums, "strip", chip)
        edges.append((near_sums, far_sums, near_halo, far_halo, ready))
    out = None
    for t in range(1, count):
        near_sums, far_sums, near_halo, far_halo, *ready = edges[t - 1]
        mids = own_mid
        for done, part in zip(cuts, middles[t - 1]):
            known = dates + done + part.shape[0]
            octets = [o for o in range(len(ready), octs) if known >= min(8 * o + 8, 2 * dates)]
            mids, *more = run(
                cross_mid_kernel,
                "cross_mid",
                (rep_mid, part, mids, near_sums, far_sums),
                (all_sums, *[eight] * len(octets)),
                work(quads_of(part.shape[0])),
                (done, octets),
            )
            ready += more
        (far_end,) = run(
            far_end_kernel,
            "far_end",
            (far_halo, far_sums, mids),
            (shape((dates + 1, 64 * octs, LANES), F32),),
            (),
        )
        block = pltpu.VMEM((dates, dates, *TILE), F32)
        (out,) = call(
            functools.partial(last_kernel, dates, count, t),
            "finish",
            (near_halo, near_sums, mids, far_end, *ready, mids if out is None else out),
            (shape((dates, dates * count, *TILE), F32),),
            (
                pltpu.VMEM((dates + 1, 64 * octs, LANES), F32),
                pltpu.VMEM((2 * dates, *TILE), F32),
                block,
                block,
                pltpu.SemaphoreType.DMA((dates,)),
            ),
            flops=5_000_000,
            hbm=True,
            aliases={4 + octs: 0} if t > 1 else None,
        )
    return out.reshape(dates, dates * count, 2, 4, LANES)


def solution(mesh):
    return jax.shard_map(
        per_device,
        mesh=mesh,
        in_specs=(P("date", None, "strip", None),),
        out_specs=P("date", None, None, "strip", None),
        check_vma=False,
    )
```

```python
import functools

import jax
import jax.numpy as jnp
from jax import lax
from jax.experimental import pallas as pl
from jax.experimental.pallas import tpu as pltpu
from jax.sharding import PartitionSpec as P

EPS = 1e-06
LANES = 128
CELL = 11
STEPS = 33
TILE = (8, LANES)
F32 = jnp.float32
VMEM = pltpu.MemorySpace.VMEM


def iota(dim):
    return lax.broadcasted_iota(jnp.int32, TILE, dim)


def put_rows(ref, date, row, flat, q, at):
    pair = ref[date, row].astype(F32)
    for m in range(CELL):
        flat[q, m, at : at + 2, :] = pair[:, m * LANES : (m + 1) * LANES]


def unpack_mid(parts, flat):
    first = 0
    for ref in parts:
        dates = ref.shape[0]

        def one(q, carry, ref=ref, dates=dates, first=first):
            for part in range(4):
                date = jnp.minimum(4 * q + part, dates - 1)
                for row in range(6):
                    put_rows(ref, date, row, flat, first + q, part * 12 + row * 2)
            return carry

        lax.fori_loop(0, quads_of(dates), one, 0)
        first += quads_of(dates)
    return first


def unpack_edge(dates, own, other, flat):
    for j in range(2 * dates):
        ref, date = (own, j) if j < dates else (other, j - dates)
        for sub in range(3):
            put_rows(ref, date, sub, flat, j // 8, (j % 8) * 6 + sub * 2)


def rotate(count, flat, cells):
    lane = iota(1)
    turn = lax.rem(lane * 3, CELL)
    bits = [(s, (turn & s) != 0) for s in (1, 2, 4, 8)]

    def one(q, carry):
        for part in range(6):
            v = [flat[q, m, pl.ds(part, 8, stride=6), :] for m in range(CELL)]
            for shift, mask in bits:
                v = [jnp.where(mask, v[(t + shift) % CELL], v[t]) for t in range(CELL)]
            for c in range(CELL):
                cells[q, part % 2, (part // 2) * CELL + c] = v[(8 * c) % CELL]
        return carry

    lax.fori_loop(0, count, one, 0)


def place(count, cells, spread=None):
    lane = iota(1)
    for c in range(CELL):
        pick = (lane * CELL + c) & (LANES - 1)

        def one(q, carry):
            for ri in range(2):
                for sub in range(3):
                    s = sub * CELL + c
                    v = jnp.take_along_axis(cells[q, ri, s], pick, axis=1)
                    cells[q, ri, s] = v
                    if spread is not None:
                        spread(q, ri, s, v)
            return carry

        lax.fori_loop(0, count, one, 0, unroll=count)


def spread_mid(rep):
    low = iota(0) < 4
    even = (iota(0) & 2) == 0

    def spread(q, ri, s, v):
        a = jnp.where(even, v, pltpu.roll(v, 2, 0))
        b = jnp.where(even, pltpu.roll(v, 6, 0), v)
        c, d = pltpu.roll(a, 4, 0), pltpu.roll(b, 4, 0)
        rep[4 * q, ri, s] = jnp.where(low, a, c)
        rep[4 * q + 1, ri, s] = jnp.where(low, b, d)
        rep[4 * q + 2, ri, s] = jnp.where(low, c, a)
        rep[4 * q + 3, ri, s] = jnp.where(low, d, b)

    return spread


def products(rows, cols, load, cells):
    count = len(rows) * len(cols)

    def step(s, acc):
        a = [load(i, 0, s) for i in rows]
        b = [load(i, 1, s) for i in rows]
        ab = [x + y for x, y in zip(a, b)]
        acc = list(acc)
        at = 0
        for q in cols:
            c, d = cells[q, 0, s], cells[q, 1, s]
            cd = c - d
            for i in range(len(rows)):
                acc[at] = acc[at] + a[i] * c
                acc[at + 1] = acc[at + 1] + b[i] * d
                acc[at + 2] = acc[at + 2] + ab[i] * cd
                at += 3
        return tuple(acc)

    acc = lax.fori_loop(0, STEPS, step, (jnp.zeros(TILE, F32),) * (3 * count), unroll=11)
    at = 0
    for j in range(len(cols)):
        for i in range(len(rows)):
            p, q, r = acc[at : at + 3]
            yield i, j, p + q, r - p + q
            at += 3


def powers(qs, cells):
    def step(s, acc):
        out = []
        for n, q in enumerate(qs):
            c, d = cells[q, 0, s], cells[q, 1, s]
            out.append(acc[n] + c * c + d * d)
        return tuple(out)

    return lax.fori_loop(0, STEPS, step, (jnp.zeros(TILE, F32),) * len(qs), unroll=11)


def quads_of(dates):
    return (dates + 3) // 4


def octs_of(dates):
    return (2 * dates + 7) // 8


def edge_kernel(dates, own, other, sums, flat, cells):
    octs = octs_of(dates)
    unpack_edge(dates, own, other, flat)
    rotate(octs, flat, cells)
    place(octs, cells)
    for o, pw in enumerate(powers(range(octs), cells)):
        sums[2 * octs * dates + o] = pw

    def load(i, ri, s):
        return cells[i // 8, ri, s, pl.ds(i % 8, 8, stride=0), :]

    for b in range(dates // 2):
        for i, o, re, im in products([2 * b, 2 * b + 1], range(octs), load, cells):
            at = 2 * octs * (2 * b + i) + o
            sums[at] = re
            sums[at + octs] = im


def near_kernel(dates, own, other, far, mids, sums, rows, flat, cells):
    edge_kernel(dates, own, other, sums, flat, cells)
    middle_rows(dates, 0, sums, far, mids, rows)


def put_mid(dates, quads, rep, cells, sums, first=0, rows=None):
    def store(n, q, v):
        size = 8 if rows is None else min(8, rows - 8 * q)
        sums[n, first + 8 * q : first + 8 * q + size, :] = v[:size]

    for q, pw in enumerate(powers(range(quads), cells)):
        store(2 * dates, q, pw)

    def one(b, carry):
        pairs = products([2 * b, 2 * b + 1], range(quads), lambda i, ri, s: rep[i, ri, s], cells)
        for i, q, re, im in pairs:
            store(4 * b + 2 * i, q, re)
            store(4 * b + 2 * i + 1, q, im)
        return carry

    lax.fori_loop(0, dates // 2, one, 0)


def own_mid_kernel(dates, *refs):
    *parts, rep, sums, flat, cells = refs
    quads = unpack_mid(parts, flat)
    rotate(quads, flat, cells)
    place(quads, cells, spread_mid(rep))
    put_mid(dates, quads, rep, cells, sums)


def cross_mid_kernel(dates, done, ready, rep, mid, before, near, far, sums, *refs):
    rows = refs[: len(ready)]
    flat, cells = refs[len(ready) :]

    def keep(n, carry):
        sums[n, : 2 * (dates + done), :] = before[n, : 2 * (dates + done), :]
        return carry

    quads = unpack_mid([mid], flat)
    rotate(quads, flat, cells)
    place(quads, cells)
    lax.fori_loop(0, 2 * dates + 1, keep, 0, unroll=3)
    put_mid(dates, quads, rep, cells, sums, 2 * (dates + done), 2 * mid.shape[0])
    for o, out in zip(ready, rows):
        middle_rows(dates, o, near, far, sums, out)


def box(v):
    lane = iota(1)
    left = jnp.where(lane > 0, pltpu.roll(v, 1, 1), 0.0)
    right = jnp.where(lane < LANES - 1, pltpu.roll(v, LANES - 1, 1), 0.0)
    return v + left + right


def odd_strip():
    return iota(0) * 0 + lax.rem(lax.axis_index("strip"), 2) == 1


def vreg_of(dates, i, comp, o):
    octs = octs_of(dates)
    if isinstance(i, int) and i == dates:
        return 2 * octs * dates + o
    return 2 * octs * i + octs * comp + o


def mids_of(dates, i, comp, o, mids):
    row = 2 * dates if isinstance(i, int) and i == dates else 2 * i + comp
    return (mids[row, pl.ds(16 * o + e, 8, stride=2), :] for e in range(2))


def each_date(dates, one):
    def step(i, carry):
        one(i)
        return carry

    one(dates)
    lax.fori_loop(0, dates, step, 0, unroll=dates)


def middle_rows(dates, o, near, far, mids, out):
    odd = odd_strip()

    def one(i):
        for comp in range(2):
            at = vreg_of(dates, i, comp, o)
            p, q = near[at], far[at]
            b, c = mids_of(dates, i, comp, o, mids)
            a, d = jnp.where(odd, p, q), jnp.where(odd, q, p)
            bc = b + c
            out[i, pl.ds(4 * comp + 1, 8, stride=8), :] = box(a + bc)
            out[i, pl.ds(4 * comp + 2, 8, stride=8), :] = box(bc + d)

    each_date(dates, one)


def outer_row(dates, i, side, sums, halo, mids, out):
    odd = odd_strip()
    for o in range(octs_of(dates)):
        for comp in range(2):
            at = vreg_of(dates, i, comp, o)
            b, c = mids_of(dates, i, comp, o, mids)
            first, second = (b, c) if side == "near" else (c, b)
            v = box(halo[at] + sums[at] + jnp.where(odd, first, second))
            for r in (0, 3):
                out[i, pl.ds(64 * o + 4 * comp + r, 8, stride=8), :] = v


def far_end_kernel(dates, far_halo, far, mids, out):
    each_date(dates, lambda i: outer_row(dates, i, "far", far, far_halo, mids, out))


def last_kernel(dates, count, turn, near_halo, near, mids, far_end, *refs):
    octs = octs_of(dates)
    middle = refs[:octs]
    before, out, ends, scale, mine, other, sem = refs[octs:]
    me = lax.axis_index("date")
    base = lax.rem(me + count - turn, count) * dates
    sub = iota(0) & 3
    odd = odd_strip()
    near_row = sub == jnp.where(odd, 0, 3)
    far_row = sub == jnp.where(odd, 3, 0)

    def tile(i, j):
        o, at = j // 8, 8 * (j % 8)
        rows = slice(8 * j, 8 * j + 8)
        rest = jnp.where(far_row, far_end[i, rows, :], middle[o][i, at : at + 8, :])
        return jnp.where(near_row, ends[i, rows, :], rest)

    each_date(dates, lambda i: outer_row(dates, i, "near", near, near_halo, mids, ends))
    for j in range(2 * dates):
        scale[j] = lax.rsqrt(tile(dates, j) + EPS)

    def copies(b):
        rows = pl.ds(2 * b, 2)
        yield pltpu.make_async_copy(other.at[rows], out.at[rows, pl.ds(base, dates)], sem.at[b])
        if turn == 1:
            own = out.at[rows, pl.ds(me * dates, dates)]
            yield pltpu.make_async_copy(mine.at[rows], own, sem.at[dates // 2 + b])

    for b in range(dates // 2):
        for i in (2 * b, 2 * b + 1):
            own = scale[i]
            for j in range(2 * dates):
                v = tile(i, j) * (own * scale[j])
                if j < dates:
                    mine[i, j] = v
                else:
                    other[i, j - dates] = v
        for copy in copies(b):
            copy.start()
    for b in range(dates // 2):
        for copy in copies(b):
            copy.wait()


def call(kernel, name, args, outs, scratch=(), flops=0, limit=32, hbm=False, aliases=None):
    vm = pl.BlockSpec(memory_space=VMEM)
    far = pl.BlockSpec(memory_space=pltpu.MemorySpace.HBM)
    ins = [vm] * len(args)
    for n in aliases or {}:
        ins[n] = far
    size = sum(a.size * a.dtype.itemsize for a in (*args, *outs))
    return pl.pallas_call(
        kernel,
        out_shape=tuple(outs),
        in_specs=ins,
        out_specs=(far if hbm else vm,) * len(outs),
        scratch_shapes=list(scratch),
        input_output_aliases=aliases or {},
        compiler_params=pltpu.CompilerParams(vmem_limit_bytes=limit << 20),
        cost_estimate=pl.CostEstimate(flops=flops, bytes_accessed=size, transcendentals=0),
        name=name,
    )(*args)


def per_device(slc):
    dates, _, rows, width = slc.shape
    count = lax.axis_size("date")
    strips = lax.axis_size("strip")
    chip = [(i, i ^ 1) for i in range(strips)]
    chips = [(i, i + 1 if i % 2 else i - 1) for i in range(1, strips - 1)]
    quads, octs = quads_of(dates), octs_of(dates)
    shape = jax.ShapeDtypeStruct
    edge_sums = shape((octs * (2 * dates + 1), *TILE), F32)
    mid_sums = shape((2 * dates + 1, 16 * ((dates + 7) // 8), LANES), F32)
    all_sums = shape((2 * dates + 1, 16 * octs, LANES), F32)
    eight = shape((dates + 1, 64, LANES), F32)
    rep = shape((4 * quads, 2, STEPS, *TILE), F32)

    def work(n):
        return pltpu.VMEM((n, CELL, 48, LANES), F32), pltpu.VMEM((n, 2, STEPS, *TILE), F32)

    def run(kernel, name, args, outs, scratch, fixed=()):
        return call(functools.partial(kernel, dates, *fixed), name, args, outs, scratch, flops=15_000_000)

    x = jnp.transpose(slc, (0, 2, 1, 3))
    odd = lax.rem(lax.axis_index("strip"), 2)
    far = lax.dynamic_slice_in_dim(x, odd * (rows - 3), 3, 1)
    x, far = lax.optimization_barrier((x, far))
    near = lax.dynamic_slice_in_dim(x, (1 - odd) * (rows - 3), 3, 1)
    cuts = [0] + [] + [dates]
    parts = [x[lo:hi, 3 : rows - 3] for lo, hi in zip(cuts, cuts[1:])]
    near, parts = lax.optimization_barrier((near, parts))
    rings = [[(i, (i + t) % count) for i in range(count)] for t in range(1, count)]
    fars = [lax.ppermute(far, "date", ring) for ring in rings]
    nears = [lax.ppermute(near, "date", ring) for ring in rings]
    middles = [[lax.ppermute(part, "date", ring) for part in parts] for ring in rings]
    edges = []
    for t in range(1, count):
        (far_sums,) = run(edge_kernel, "far_pairs", (far, fars[t - 1]), (edge_sums,), work(octs))
        far_halo = lax.ppermute(far_sums, "strip", chips)
        if t == 1:
            own_rows, far_sums = lax.optimization_barrier((parts, far_sums))
            rep_mid, own_mid = run(own_mid_kernel, "own_mid", own_rows, (rep, mid_sums), work(quads))
            nears, rep_mid = lax.optimization_barrier((nears, rep_mid))
        args = (near, nears[t - 1], far_sums, own_mid)
        near_sums, ready = run(near_kernel, "near_pairs", args, (edge_sums, eight), work(octs))
        near_halo = lax.ppermute(near_sums, "strip", chip)
        edges.append((near_sums, far_sums, near_halo, far_halo, ready))
    out = None
    for t in range(1, count):
        near_sums, far_sums, near_halo, far_halo, *ready = edges[t - 1]
        mids = own_mid
        for done, part in zip(cuts, middles[t - 1]):
            known = dates + done + part.shape[0]
            octets = [o for o in range(len(ready), octs) if known >= min(8 * o + 8, 2 * dates)]
            mids, *more = run(
                cross_mid_kernel,
                "cross_mid",
                (rep_mid, part, mids, near_sums, far_sums),
                (all_sums, *[eight] * len(octets)),
                work(quads_of(part.shape[0])),
                (done, octets),
            )
            ready += more
        (far_end,) = run(
            far_end_kernel,
            "far_end",
            (far_halo, far_sums, mids),
            (shape((dates + 1, 64 * octs, LANES), F32),),
            (),
        )
        block = pltpu.VMEM((dates, dates, *TILE), F32)
        (out,) = call(
            functools.partial(last_kernel, dates, count, t),
            "finish",
            (near_halo, near_sums, mids, far_end, *ready, mids if out is None else out),
            (shape((dates, dates * count, *TILE), F32),),
            (
                pltpu.VMEM((dates + 1, 64 * octs, LANES), F32),
                pltpu.VMEM((2 * dates, *TILE), F32),
                block,
                block,
                pltpu.SemaphoreType.DMA((dates,)),
            ),
            flops=5_000_000,
            hbm=True,
            aliases={4 + octs: 0} if t > 1 else None,
        )
    return out.reshape(dates, dates * count, 2, 4, LANES)


def solution(mesh):
    return jax.shard_map(
        per_device,
        mesh=mesh,
        in_specs=(P("date", None, "strip", None),),
        out_specs=P("date", None, None, "strip", None),
        check_vma=False,
    )
```

```python
import functools

import jax
import jax.numpy as jnp
from jax import lax
from jax.experimental import pallas as pl
from jax.experimental.pallas import tpu as pltpu
from jax.sharding import PartitionSpec as P

EPS = 1e-06
LANES = 128
CELL = 11
STEPS = 33
TILE = (8, LANES)
F32 = jnp.float32
VMEM = pltpu.MemorySpace.VMEM


def iota(dim):
    return lax.broadcasted_iota(jnp.int32, TILE, dim)


def put_rows(ref, date, row, flat, q, at):
    pair = ref[date, row].astype(F32)
    for m in range(CELL):
        flat[q, m, at : at + 2, :] = pair[:, m * LANES : (m + 1) * LANES]


def unpack_mid(parts, flat):
    first = 0
    for ref in parts:
        dates = ref.shape[0]

        def one(q, carry, ref=ref, dates=dates, first=first):
            for part in range(4):
                date = jnp.minimum(4 * q + part, dates - 1)
                for row in range(6):
                    put_rows(ref, date, row, flat, first + q, part * 12 + row * 2)
            return carry

        lax.fori_loop(0, quads_of(dates), one, 0)
        first += quads_of(dates)
    return first


def unpack_edge(dates, own, other, flat):
    for j in range(2 * dates):
        ref, date = (own, j) if j < dates else (other, j - dates)
        for sub in range(3):
            put_rows(ref, date, sub, flat, j // 8, (j % 8) * 6 + sub * 2)


def rotate(count, flat, cells):
    lane = iota(1)
    turn = lax.rem(lane * 3, CELL)
    bits = [(s, (turn & s) != 0) for s in (1, 2, 4, 8)]

    def one(q, carry):
        for part in range(6):
            v = [flat[q, m, pl.ds(part, 8, stride=6), :] for m in range(CELL)]
            for shift, mask in bits:
                v = [jnp.where(mask, v[(t + shift) % CELL], v[t]) for t in range(CELL)]
            for c in range(CELL):
                cells[q, part % 2, (part // 2) * CELL + c] = v[(8 * c) % CELL]
        return carry

    lax.fori_loop(0, count, one, 0)


def place(count, cells, spread=None):
    lane = iota(1)
    for c in range(CELL):
        pick = (lane * CELL + c) & (LANES - 1)

        def one(q, carry):
            for ri in range(2):
                for sub in range(3):
                    s = sub * CELL + c
                    v = jnp.take_along_axis(cells[q, ri, s], pick, axis=1)
                    cells[q, ri, s] = v
                    if spread is not None:
                        spread(q, ri, s, v)
            return carry

        lax.fori_loop(0, count, one, 0, unroll=count)


def spread_mid(rep):
    low = iota(0) < 4
    even = (iota(0) & 2) == 0

    def spread(q, ri, s, v):
        a = jnp.where(even, v, pltpu.roll(v, 2, 0))
        b = jnp.where(even, pltpu.roll(v, 6, 0), v)
        c, d = pltpu.roll(a, 4, 0), pltpu.roll(b, 4, 0)
        rep[4 * q, ri, s] = jnp.where(low, a, c)
        rep[4 * q + 1, ri, s] = jnp.where(low, b, d)
        rep[4 * q + 2, ri, s] = jnp.where(low, c, a)
        rep[4 * q + 3, ri, s] = jnp.where(low, d, b)

    return spread


def products(rows, cols, load, cells):
    count = len(rows) * len(cols)

    def step(s, acc):
        a = [load(i, 0, s) for i in rows]
        b = [load(i, 1, s) for i in rows]
        ab = [x + y for x, y in zip(a, b)]
        acc = list(acc)
        at = 0
        for q in cols:
            c, d = cells[q, 0, s], cells[q, 1, s]
            cd = c - d
            for i in range(len(rows)):
                acc[at] = acc[at] + a[i] * c
                acc[at + 1] = acc[at + 1] + b[i] * d
                acc[at + 2] = acc[at + 2] + ab[i] * cd
                at += 3
        return tuple(acc)

    acc = lax.fori_loop(0, STEPS, step, (jnp.zeros(TILE, F32),) * (3 * count), unroll=11)
    at = 0
    for j in range(len(cols)):
        for i in range(len(rows)):
            p, q, r = acc[at : at + 3]
            yield i, j, p + q, r - p + q
            at += 3


def powers(qs, cells):
    def step(s, acc):
        out = []
        for n, q in enumerate(qs):
            c, d = cells[q, 0, s], cells[q, 1, s]
            out.append(acc[n] + c * c + d * d)
        return tuple(out)

    return lax.fori_loop(0, STEPS, step, (jnp.zeros(TILE, F32),) * len(qs), unroll=11)


def quads_of(dates):
    return (dates + 3) // 4


def octs_of(dates):
    return (2 * dates + 7) // 8


def edge_kernel(dates, own, other, sums, flat, cells):
    octs = octs_of(dates)
    unpack_edge(dates, own, other, flat)
    rotate(octs, flat, cells)
    place(octs, cells)
    for o, pw in enumerate(powers(range(octs), cells)):
        sums[2 * octs * dates + o] = pw

    def load(i, ri, s):
        return cells[i // 8, ri, s, pl.ds(i % 8, 8, stride=0), :]

    for b in range(dates // 2):
        for i, o, re, im in products([2 * b, 2 * b + 1], range(octs), load, cells):
            at = 2 * octs * (2 * b + i) + o
            sums[at] = re
            sums[at + octs] = im


def near_kernel(dates, own, other, far, mids, sums, rows, flat, cells):
    edge_kernel(dates, own, other, sums, flat, cells)
    middle_rows(dates, 0, sums, far, mids, rows)


def put_mid(dates, quads, rep, cells, sums, first=0, rows=None):
    def store(n, q, v):
        size = 8 if rows is None else min(8, rows - 8 * q)
        sums[n, first + 8 * q : first + 8 * q + size, :] = v[:size]

    for q, pw in enumerate(powers(range(quads), cells)):
        store(2 * dates, q, pw)

    def one(b, carry):
        pairs = products([2 * b, 2 * b + 1], range(quads), lambda i, ri, s: rep[i, ri, s], cells)
        for i, q, re, im in pairs:
            store(4 * b + 2 * i, q, re)
            store(4 * b + 2 * i + 1, q, im)
        return carry

    lax.fori_loop(0, dates // 2, one, 0)


def own_mid_kernel(dates, *refs):
    *parts, rep, sums, flat, cells = refs
    quads = unpack_mid(parts, flat)
    rotate(quads, flat, cells)
    place(quads, cells, spread_mid(rep))
    put_mid(dates, quads, rep, cells, sums)


def cross_mid_kernel(dates, first, kept, ready, rep, mid, before, near, far, sums, *refs):
    rows = refs[: len(ready)]
    flat, cells = refs[len(ready) :]

    def keep(n, carry):
        sums[n, :kept, :] = before[n, :kept, :]
        return carry

    quads = unpack_mid([mid], flat)
    rotate(quads, flat, cells)
    place(quads, cells)
    lax.fori_loop(0, 2 * dates + 1, keep, 0, unroll=3)
    put_mid(dates, quads, rep, cells, sums, 2 * (dates + first), 2 * mid.shape[0])
    for o, out in zip(ready, rows):
        middle_rows(dates, o, near, far, sums, out)


def box(v):
    lane = iota(1)
    left = jnp.where(lane > 0, pltpu.roll(v, 1, 1), 0.0)
    right = jnp.where(lane < LANES - 1, pltpu.roll(v, LANES - 1, 1), 0.0)
    return v + left + right


def odd_strip():
    return iota(0) * 0 + lax.rem(lax.axis_index("strip"), 2) == 1


def vreg_of(dates, i, comp, o):
    octs = octs_of(dates)
    if isinstance(i, int) and i == dates:
        return 2 * octs * dates + o
    return 2 * octs * i + octs * comp + o


def mids_of(dates, i, comp, o, mids):
    row = 2 * dates if isinstance(i, int) and i == dates else 2 * i + comp
    return (mids[row, pl.ds(16 * o + e, 8, stride=2), :] for e in range(2))


def each_date(dates, one):
    def step(i, carry):
        one(i)
        return carry

    one(dates)
    lax.fori_loop(0, dates, step, 0, unroll=dates)


def middle_rows(dates, o, near, far, mids, out):
    odd = odd_strip()

    def one(i):
        for comp in range(2):
            at = vreg_of(dates, i, comp, o)
            p, q = near[at], far[at]
            b, c = mids_of(dates, i, comp, o, mids)
            a, d = jnp.where(odd, p, q), jnp.where(odd, q, p)
            bc = b + c
            out[i, pl.ds(4 * comp + 1, 8, stride=8), :] = box(a + bc)
            out[i, pl.ds(4 * comp + 2, 8, stride=8), :] = box(bc + d)

    each_date(dates, one)


def outer_row(dates, i, side, sums, halo, mids, out):
    odd = odd_strip()
    for o in range(octs_of(dates)):
        for comp in range(2):
            at = vreg_of(dates, i, comp, o)
            b, c = mids_of(dates, i, comp, o, mids)
            first, second = (b, c) if side == "near" else (c, b)
            v = box(halo[at] + sums[at] + jnp.where(odd, first, second))
            for r in (0, 3):
                out[i, pl.ds(64 * o + 4 * comp + r, 8, stride=8), :] = v


def far_end_kernel(dates, far_halo, far, mids, out):
    each_date(dates, lambda i: outer_row(dates, i, "far", far, far_halo, mids, out))


def last_kernel(dates, count, turn, near_halo, near, mids, far_end, *refs):
    octs = octs_of(dates)
    middle = refs[:octs]
    before, out, ends, scale, mine, other, sem = refs[octs:]
    me = lax.axis_index("date")
    base = lax.rem(me + count - turn, count) * dates
    sub = iota(0) & 3
    odd = odd_strip()
    near_row = sub == jnp.where(odd, 0, 3)
    far_row = sub == jnp.where(odd, 3, 0)

    def tile(i, j):
        o, at = j // 8, 8 * (j % 8)
        rows = slice(8 * j, 8 * j + 8)
        rest = jnp.where(far_row, far_end[i, rows, :], middle[o][i, at : at + 8, :])
        return jnp.where(near_row, ends[i, rows, :], rest)

    each_date(dates, lambda i: outer_row(dates, i, "near", near, near_halo, mids, ends))
    for j in range(2 * dates):
        scale[j] = lax.rsqrt(tile(dates, j) + EPS)

    def copies(b):
        rows = pl.ds(2 * b, 2)
        yield pltpu.make_async_copy(other.at[rows], out.at[rows, pl.ds(base, dates)], sem.at[b])
        if turn == 1:
            own = out.at[rows, pl.ds(me * dates, dates)]
            yield pltpu.make_async_copy(mine.at[rows], own, sem.at[dates // 2 + b])

    for b in range(dates // 2):
        for i in (2 * b, 2 * b + 1):
            own = scale[i]
            for j in range(2 * dates):
                v = tile(i, j) * (own * scale[j])
                if j < dates:
                    mine[i, j] = v
                else:
                    other[i, j - dates] = v
        for copy in copies(b):
            copy.start()
    for b in range(dates // 2):
        for copy in copies(b):
            copy.wait()


def call(kernel, name, args, outs, scratch=(), flops=0, limit=32, hbm=False, aliases=None):
    vm = pl.BlockSpec(memory_space=VMEM)
    far = pl.BlockSpec(memory_space=pltpu.MemorySpace.HBM)
    ins = [vm] * len(args)
    for n in aliases or {}:
        ins[n] = far
    size = sum(a.size * a.dtype.itemsize for a in (*args, *outs))
    return pl.pallas_call(
        kernel,
        out_shape=tuple(outs),
        in_specs=ins,
        out_specs=(far if hbm else vm,) * len(outs),
        scratch_shapes=list(scratch),
        input_output_aliases=aliases or {},
        compiler_params=pltpu.CompilerParams(vmem_limit_bytes=limit << 20),
        cost_estimate=pl.CostEstimate(flops=flops, bytes_accessed=size, transcendentals=0),
        name=name,
    )(*args)


def per_device(slc):
    dates, _, rows, width = slc.shape
    count = lax.axis_size("date")
    strips = lax.axis_size("strip")
    chip = [(i, i ^ 1) for i in range(strips)]
    chips = [(i, i + 1 if i % 2 else i - 1) for i in range(1, strips - 1)]
    quads, octs = quads_of(dates), octs_of(dates)
    shape = jax.ShapeDtypeStruct
    edge_sums = shape((octs * (2 * dates + 1), *TILE), F32)
    mid_sums = shape((2 * dates + 1, 16 * ((dates + 7) // 8), LANES), F32)
    all_sums = shape((2 * dates + 1, 16 * octs, LANES), F32)
    eight = shape((dates + 1, 64, LANES), F32)
    rep = shape((4 * quads, 2, STEPS, *TILE), F32)

    def work(n):
        return pltpu.VMEM((n, CELL, 48, LANES), F32), pltpu.VMEM((n, 2, STEPS, *TILE), F32)

    def run(kernel, name, args, outs, scratch, fixed=()):
        return call(functools.partial(kernel, dates, *fixed), name, args, outs, scratch, flops=15_000_000)

    x = jnp.transpose(slc, (0, 2, 1, 3))
    odd = lax.rem(lax.axis_index("strip"), 2)
    far = lax.dynamic_slice_in_dim(x, odd * (rows - 3), 3, 1)
    x, far = lax.optimization_barrier((x, far))
    near = lax.dynamic_slice_in_dim(x, (1 - odd) * (rows - 3), 3, 1)
    spans = [(0, 8), (8, dates)]
    parts = [x[lo:hi, 3 : rows - 3] for lo, hi in spans]
    near, parts = lax.optimization_barrier((near, parts))
    rings = [[(i, (i + t) % count) for i in range(count)] for t in range(1, count)]
    fars = [lax.ppermute(far, "date", ring) for ring in rings]
    nears = [lax.ppermute(near, "date", ring) for ring in rings]
    middles = [[lax.ppermute(part, "date", ring) for part in parts] for ring in rings]
    edges = []
    for t in range(1, count):
        (far_sums,) = run(edge_kernel, "far_pairs", (far, fars[t - 1]), (edge_sums,), work(octs))
        far_halo = lax.ppermute(far_sums, "strip", chips)
        if t == 1:
            own_rows, far_sums = lax.optimization_barrier((parts, far_sums))
            rep_mid, own_mid = run(own_mid_kernel, "own_mid", own_rows, (rep, mid_sums), work(quads))
            early = [part[1] for part in middles]
            nears, early, rep_mid = lax.optimization_barrier((nears, early, rep_mid))
        args = (near, nears[t - 1], far_sums, own_mid)
        near_sums, ready = run(near_kernel, "near_pairs", args, (edge_sums, eight), work(octs))
        near_halo = lax.ppermute(near_sums, "strip", chip)
        edges.append((near_sums, far_sums, near_halo, far_halo, ready))
    out = None
    for t in range(1, count):
        near_sums, far_sums, near_halo, far_halo, ready = edges[t - 1]
        middle = {0: ready}
        known = set(range(dates))
        mids, kept = own_mid, 2 * dates
        for (lo, hi), part in ((spans[1], early[t - 1]), (spans[0], middles[t - 1][0])):
            known |= set(range(dates + lo, dates + hi))
            slots = {o: range(8 * o, min(8 * o + 8, 2 * dates)) for o in range(octs)}
            octets = [o for o in slots if o not in middle and known.issuperset(slots[o])]
            mids, *more = run(
                cross_mid_kernel,
                "cross_mid",
                (rep_mid, part, mids, near_sums, far_sums),
                (all_sums, *[eight] * len(octets)),
                work(quads_of(hi - lo)),
                (lo, kept, octets),
            )
            middle.update(zip(octets, more))
            kept = 4 * dates
        ready = [middle[o] for o in range(octs)]
        (far_end,) = run(
            far_end_kernel,
            "far_end",
            (far_halo, far_sums, mids),
            (shape((dates + 1, 64 * octs, LANES), F32),),
            (),
        )
        block = pltpu.VMEM((dates, dates, *TILE), F32)
        (out,) = call(
            functools.partial(last_kernel, dates, count, t),
            "finish",
            (near_halo, near_sums, mids, far_end, *ready, mids if out is None else out),
            (shape((dates, dates * count, *TILE), F32),),
            (
                pltpu.VMEM((dates + 1, 64 * octs, LANES), F32),
                pltpu.VMEM((2 * dates, *TILE), F32),
                block,
                block,
                pltpu.SemaphoreType.DMA((dates,)),
            ),
            flops=5_000_000,
            hbm=True,
            aliases={4 + octs: 0} if t > 1 else None,
        )
    return out.reshape(dates, dates * count, 2, 4, LANES)


def solution(mesh):
    return jax.shard_map(
        per_device,
        mesh=mesh,
        in_specs=(P("date", None, "strip", None),),
        out_specs=P("date", None, None, "strip", None),
        check_vma=False,
    )
```

```python
import functools

import jax
import jax.numpy as jnp
from jax import lax
from jax.experimental import pallas as pl
from jax.experimental.pallas import tpu as pltpu
from jax.sharding import PartitionSpec as P

EPS = 1e-06
LANES = 128
CELL = 11
STEPS = 33
TILE = (8, LANES)
F32 = jnp.float32
VMEM = pltpu.MemorySpace.VMEM


def iota(dim):
    return lax.broadcasted_iota(jnp.int32, TILE, dim)


def put_rows(ref, date, row, flat, q, at):
    pair = ref[date, row].astype(F32)
    for m in range(CELL):
        flat[q, m, at : at + 2, :] = pair[:, m * LANES : (m + 1) * LANES]


def unpack_mid(parts, flat):
    first = 0
    for ref in parts:
        dates = ref.shape[0]

        def one(q, carry, ref=ref, dates=dates, first=first):
            for part in range(4):
                date = jnp.minimum(4 * q + part, dates - 1)
                for row in range(6):
                    put_rows(ref, date, row, flat, first + q, part * 12 + row * 2)
            return carry

        lax.fori_loop(0, quads_of(dates), one, 0)
        first += quads_of(dates)
    return first


def unpack_edge(dates, own, other, flat):
    for j in range(2 * dates):
        ref, date = (own, j) if j < dates else (other, j - dates)
        for sub in range(3):
            put_rows(ref, date, sub, flat, j // 8, (j % 8) * 6 + sub * 2)


def rotate(count, flat, cells):
    lane = iota(1)
    turn = lax.rem(lane * 3, CELL)
    bits = [(s, (turn & s) != 0) for s in (1, 2, 4, 8)]

    def one(q, carry):
        for part in range(6):
            v = [flat[q, m, pl.ds(part, 8, stride=6), :] for m in range(CELL)]
            for shift, mask in bits:
                v = [jnp.where(mask, v[(t + shift) % CELL], v[t]) for t in range(CELL)]
            for c in range(CELL):
                cells[q, part % 2, (part // 2) * CELL + c] = v[(8 * c) % CELL]
        return carry

    lax.fori_loop(0, count, one, 0)


def place(count, cells, spread=None):
    lane = iota(1)
    for c in range(CELL):
        pick = (lane * CELL + c) & (LANES - 1)

        def one(q, carry):
            for ri in range(2):
                for sub in range(3):
                    s = sub * CELL + c
                    v = jnp.take_along_axis(cells[q, ri, s], pick, axis=1)
                    cells[q, ri, s] = v
                    if spread is not None:
                        spread(q, ri, s, v)
            return carry

        lax.fori_loop(0, count, one, 0, unroll=count)


def spread_mid(rep):
    low = iota(0) < 4
    even = (iota(0) & 2) == 0

    def spread(q, ri, s, v):
        a = jnp.where(even, v, pltpu.roll(v, 2, 0))
        b = jnp.where(even, pltpu.roll(v, 6, 0), v)
        c, d = pltpu.roll(a, 4, 0), pltpu.roll(b, 4, 0)
        rep[4 * q, ri, s] = jnp.where(low, a, c)
        rep[4 * q + 1, ri, s] = jnp.where(low, b, d)
        rep[4 * q + 2, ri, s] = jnp.where(low, c, a)
        rep[4 * q + 3, ri, s] = jnp.where(low, d, b)

    return spread


def products(rows, cols, load, cells):
    count = len(rows) * len(cols)

    def step(s, acc):
        a = [load(i, 0, s) for i in rows]
        b = [load(i, 1, s) for i in rows]
        ab = [x + y for x, y in zip(a, b)]
        acc = list(acc)
        at = 0
        for q in cols:
            c, d = cells[q, 0, s], cells[q, 1, s]
            cd = c - d
            for i in range(len(rows)):
                acc[at] = acc[at] + a[i] * c
                acc[at + 1] = acc[at + 1] + b[i] * d
                acc[at + 2] = acc[at + 2] + ab[i] * cd
                at += 3
        return tuple(acc)

    acc = lax.fori_loop(0, STEPS, step, (jnp.zeros(TILE, F32),) * (3 * count), unroll=11)
    at = 0
    for j in range(len(cols)):
        for i in range(len(rows)):
            p, q, r = acc[at : at + 3]
            yield i, j, p + q, r - p + q
            at += 3


def powers(qs, cells):
    def step(s, acc):
        out = []
        for n, q in enumerate(qs):
            c, d = cells[q, 0, s], cells[q, 1, s]
            out.append(acc[n] + c * c + d * d)
        return tuple(out)

    return lax.fori_loop(0, STEPS, step, (jnp.zeros(TILE, F32),) * len(qs), unroll=11)


def quads_of(dates):
    return (dates + 3) // 4


def octs_of(dates):
    return (2 * dates + 7) // 8


def edge_kernel(dates, own, other, sums, flat, cells):
    octs = octs_of(dates)
    unpack_edge(dates, own, other, flat)
    rotate(octs, flat, cells)
    place(octs, cells)
    for o, pw in enumerate(powers(range(octs), cells)):
        sums[2 * octs * dates + o] = pw

    def load(i, ri, s):
        return cells[i // 8, ri, s, pl.ds(i % 8, 8, stride=0), :]

    for b in range(dates // 2):
        for i, o, re, im in products([2 * b, 2 * b + 1], range(octs), load, cells):
            at = 2 * octs * (2 * b + i) + o
            sums[at] = re
            sums[at + octs] = im


def near_kernel(dates, own, other, far, mids, sums, rows, flat, cells):
    edge_kernel(dates, own, other, sums, flat, cells)
    middle_rows(dates, 0, sums, far, mids, rows)


def put_mid(dates, quads, rep, cells, sums, first=0, rows=None):
    def store(n, q, v):
        size = 8 if rows is None else min(8, rows - 8 * q)
        sums[n, first + 8 * q : first + 8 * q + size, :] = v[:size]

    for q, pw in enumerate(powers(range(quads), cells)):
        store(2 * dates, q, pw)

    def one(b, carry):
        pairs = products([2 * b, 2 * b + 1], range(quads), lambda i, ri, s: rep[i, ri, s], cells)
        for i, q, re, im in pairs:
            store(4 * b + 2 * i, q, re)
            store(4 * b + 2 * i + 1, q, im)
        return carry

    lax.fori_loop(0, dates // 2, one, 0)


def own_mid_kernel(dates, *refs):
    *parts, rep, sums, flat, cells = refs
    quads = unpack_mid(parts, flat)
    rotate(quads, flat, cells)
    place(quads, cells, spread_mid(rep))
    put_mid(dates, quads, rep, cells, sums)


def cross_mid_kernel(dates, done, ready, rep, mid, before, near, far, sums, *refs):
    rows = refs[: len(ready)]
    flat, cells = refs[len(ready) :]

    def keep(n, carry):
        sums[n, : 2 * (dates + done), :] = before[n, : 2 * (dates + done), :]
        return carry

    quads = unpack_mid([mid], flat)
    rotate(quads, flat, cells)
    place(quads, cells)
    lax.fori_loop(0, 2 * dates + 1, keep, 0, unroll=3)
    put_mid(dates, quads, rep, cells, sums, 2 * (dates + done), 2 * mid.shape[0])
    for o, out in zip(ready, rows):
        middle_rows(dates, o, near, far, sums, out)


def box(v):
    lane = iota(1)
    left = jnp.where(lane > 0, pltpu.roll(v, 1, 1), 0.0)
    right = jnp.where(lane < LANES - 1, pltpu.roll(v, LANES - 1, 1), 0.0)
    return v + left + right


def odd_strip():
    return iota(0) * 0 + lax.rem(lax.axis_index("strip"), 2) == 1


def vreg_of(dates, i, comp, o):
    octs = octs_of(dates)
    if isinstance(i, int) and i == dates:
        return 2 * octs * dates + o
    return 2 * octs * i + octs * comp + o


def mids_of(dates, i, comp, o, mids):
    row = 2 * dates if isinstance(i, int) and i == dates else 2 * i + comp
    return (mids[row, pl.ds(16 * o + e, 8, stride=2), :] for e in range(2))


def each_date(dates, one):
    def step(i, carry):
        one(i)
        return carry

    one(dates)
    lax.fori_loop(0, dates, step, 0, unroll=dates)


def middle_rows(dates, o, near, far, mids, out):
    odd = odd_strip()

    def one(i):
        for comp in range(2):
            at = vreg_of(dates, i, comp, o)
            p, q = near[at], far[at]
            b, c = mids_of(dates, i, comp, o, mids)
            a, d = jnp.where(odd, p, q), jnp.where(odd, q, p)
            bc = b + c
            out[i, pl.ds(4 * comp + 1, 8, stride=8), :] = box(a + bc)
            out[i, pl.ds(4 * comp + 2, 8, stride=8), :] = box(bc + d)

    each_date(dates, one)


def outer_row(dates, i, side, sums, halo, mids, out):
    odd = odd_strip()
    for o in range(octs_of(dates)):
        for comp in range(2):
            at = vreg_of(dates, i, comp, o)
            b, c = mids_of(dates, i, comp, o, mids)
            first, second = (b, c) if side == "near" else (c, b)
            v = box(halo[at] + sums[at] + jnp.where(odd, first, second))
            for r in (0, 3):
                out[i, pl.ds(64 * o + 4 * comp + r, 8, stride=8), :] = v


def far_end_kernel(dates, far_halo, far, mids, out):
    each_date(dates, lambda i: outer_row(dates, i, "far", far, far_halo, mids, out))


def last_kernel(dates, count, turn, near_halo, near, mids, far_end, *refs):
    octs = octs_of(dates)
    middle = refs[:octs]
    before, out, ends, scale, mine, other, sem = refs[octs:]
    me = lax.axis_index("date")
    base = lax.rem(me + count - turn, count) * dates
    sub = iota(0) & 3
    odd = odd_strip()
    near_row = sub == jnp.where(odd, 0, 3)
    far_row = sub == jnp.where(odd, 3, 0)

    def tile(i, j):
        o, at = j // 8, 8 * (j % 8)
        rows = slice(8 * j, 8 * j + 8)
        rest = jnp.where(far_row, far_end[i, rows, :], middle[o][i, at : at + 8, :])
        return jnp.where(near_row, ends[i, rows, :], rest)

    each_date(dates, lambda i: outer_row(dates, i, "near", near, near_halo, mids, ends))
    for j in range(2 * dates):
        scale[j] = lax.rsqrt(tile(dates, j) + EPS)

    def copies(b):
        rows = pl.ds(2 * b, 2)
        yield pltpu.make_async_copy(other.at[rows], out.at[rows, pl.ds(base, dates)], sem.at[b])
        if turn == 1:
            own = out.at[rows, pl.ds(me * dates, dates)]
            yield pltpu.make_async_copy(mine.at[rows], own, sem.at[dates // 2 + b])

    for b in range(dates // 2):
        for i in (2 * b, 2 * b + 1):
            own = scale[i]
            for j in range(2 * dates):
                v = tile(i, j) * (own * scale[j])
                if j < dates:
                    mine[i, j] = v
                else:
                    other[i, j - dates] = v
        for copy in copies(b):
            copy.start()
    for b in range(dates // 2):
        for copy in copies(b):
            copy.wait()


def far_rows_kernel(x, far, sem):
    odd = lax.rem(lax.axis_index("strip"), 2)
    copy = pltpu.make_async_copy(x.at[:, pl.ds(odd * (x.shape[1] - 3), 3)], far, sem)
    copy.start()
    copy.wait()


def other_rows_kernel(x, far, near, mid, sem):
    rows = x.shape[1]
    odd = lax.rem(lax.axis_index("strip"), 2)
    copies = [
        pltpu.make_async_copy(x.at[:, pl.ds((1 - odd) * (rows - 3), 3)], near, sem.at[0]),
        pltpu.make_async_copy(x.at[:, 3 : rows - 3], mid, sem.at[1]),
    ]
    for copy in copies:
        copy.start()
    for copy in copies:
        copy.wait()


def call(kernel, name, args, outs, scratch=(), flops=0, limit=32, hbm=False, aliases=None):
    vm = pl.BlockSpec(memory_space=VMEM)
    far = pl.BlockSpec(memory_space=pltpu.MemorySpace.HBM)
    ins = [vm] * len(args)
    for n in aliases or {}:
        ins[n] = far
    size = sum(a.size * a.dtype.itemsize for a in (*args, *outs))
    return pl.pallas_call(
        kernel,
        out_shape=tuple(outs),
        in_specs=ins,
        out_specs=(far if hbm else vm,) * len(outs),
        scratch_shapes=list(scratch),
        input_output_aliases=aliases or {},
        compiler_params=pltpu.CompilerParams(vmem_limit_bytes=limit << 20),
        cost_estimate=pl.CostEstimate(flops=flops, bytes_accessed=size, transcendentals=0),
        name=name,
    )(*args)


def per_device(slc):
    dates, _, rows, width = slc.shape
    count = lax.axis_size("date")
    strips = lax.axis_size("strip")
    chip = [(i, i ^ 1) for i in range(strips)]
    chips = [(i, i + 1 if i % 2 else i - 1) for i in range(1, strips - 1)]
    quads, octs = quads_of(dates), octs_of(dates)
    shape = jax.ShapeDtypeStruct
    edge_sums = shape((octs * (2 * dates + 1), *TILE), F32)
    mid_sums = shape((2 * dates + 1, 16 * ((dates + 7) // 8), LANES), F32)
    all_sums = shape((2 * dates + 1, 16 * octs, LANES), F32)
    eight = shape((dates + 1, 64, LANES), F32)
    rep = shape((4 * quads, 2, STEPS, *TILE), F32)

    def work(n):
        return pltpu.VMEM((n, CELL, 48, LANES), F32), pltpu.VMEM((n, 2, STEPS, *TILE), F32)

    def run(kernel, name, args, outs, scratch, fixed=()):
        return call(functools.partial(kernel, dates, *fixed), name, args, outs, scratch, flops=15_000_000)

    x = jnp.transpose(slc, (0, 2, 1, 3))
    edge = shape((dates, 3, 2, width), slc.dtype)
    vm = pl.BlockSpec(memory_space=VMEM)
    hbm = pl.BlockSpec(memory_space=pltpu.MemorySpace.HBM)
    params = pltpu.CompilerParams(vmem_limit_bytes=2 << 20)
    far = pl.pallas_call(
        far_rows_kernel,
        out_shape=edge,
        in_specs=[hbm],
        out_specs=vm,
        scratch_shapes=[pltpu.SemaphoreType.DMA],
        compiler_params=params,
        name="far_rows",
    )(x)
    near, mid = pl.pallas_call(
        other_rows_kernel,
        out_shape=(edge, shape((dates, rows - 6, 2, width), slc.dtype)),
        in_specs=[hbm, vm],
        out_specs=(vm, vm),
        scratch_shapes=[pltpu.SemaphoreType.DMA((2,))],
        compiler_params=params,
        name="other_rows",
    )(x, far)
    parts = [mid]
    cuts = [0, dates]
    rings = [[(i, (i + t) % count) for i in range(count)] for t in range(1, count)]
    fars = [lax.ppermute(far, "date", ring) for ring in rings]
    nears = [lax.ppermute(near, "date", ring) for ring in rings]
    middles = [[lax.ppermute(part, "date", ring) for part in parts] for ring in rings]
    edges = []
    for t in range(1, count):
        (far_sums,) = run(edge_kernel, "far_pairs", (far, fars[t - 1]), (edge_sums,), work(octs))
        far_halo = lax.ppermute(far_sums, "strip", chips)
        if t == 1:
            own_rows, far_sums = lax.optimization_barrier((parts, far_sums))
            rep_mid, own_mid = run(own_mid_kernel, "own_mid", own_rows, (rep, mid_sums), work(quads))
            nears, rep_mid = lax.optimization_barrier((nears, rep_mid))
        args = (near, nears[t - 1], far_sums, own_mid)
        near_sums, ready = run(near_kernel, "near_pairs", args, (edge_sums, eight), work(octs))
        near_halo = lax.ppermute(near_sums, "strip", chip)
        edges.append((near_sums, far_sums, near_halo, far_halo, ready))
    out = None
    for t in range(1, count):
        near_sums, far_sums, near_halo, far_halo, *ready = edges[t - 1]
        mids = own_mid
        for done, part in zip(cuts, middles[t - 1]):
            known = dates + done + part.shape[0]
            octets = [o for o in range(len(ready), octs) if known >= min(8 * o + 8, 2 * dates)]
            mids, *more = run(
                cross_mid_kernel,
                "cross_mid",
                (rep_mid, part, mids, near_sums, far_sums),
                (all_sums, *[eight] * len(octets)),
                work(quads_of(part.shape[0])),
                (done, octets),
            )
            ready += more
        (far_end,) = run(
            far_end_kernel,
            "far_end",
            (far_halo, far_sums, mids),
            (shape((dates + 1, 64 * octs, LANES), F32),),
            (),
        )
        block = pltpu.VMEM((dates, dates, *TILE), F32)
        (out,) = call(
            functools.partial(last_kernel, dates, count, t),
            "finish",
            (near_halo, near_sums, mids, far_end, *ready, mids if out is None else out),
            (shape((dates, dates * count, *TILE), F32),),
            (
                pltpu.VMEM((dates + 1, 64 * octs, LANES), F32),
                pltpu.VMEM((2 * dates, *TILE), F32),
                block,
                block,
                pltpu.SemaphoreType.DMA((dates,)),
            ),
            flops=5_000_000,
            hbm=True,
            aliases={4 + octs: 0} if t > 1 else None,
        )
    return out.reshape(dates, dates * count, 2, 4, LANES)


def solution(mesh):
    return jax.shard_map(
        per_device,
        mesh=mesh,
        in_specs=(P("date", None, "strip", None),),
        out_specs=P("date", None, None, "strip", None),
        check_vma=False,
    )
```
